256 devices in a mesh: slab: 8 (over x, core), coil: 32 (over y, z).
Axes of the slice: x: 4, y: 4, z: 8, core: 2. Of those that a mesh axis runs over, the one named last changes fastest.
Arguments:
- prior_image: float32 [256, 128, 128], P(('slab', 'coil')), may hold values from -12 to 12
- coil_maps: bfloat16 [32, 256, 128, 128], P('coil', 'slab'), may hold values from -3 to 3
- kspace: bfloat16 [32, 128, 256, 128], P('coil', 'slab'), may hold values from -6 to 6
- sampling: int32 [128, 256], P('slab'), may hold values 0 or 1
- weight_first: bfloat16 [3, 3, 3, 32, 2], replicated, may hold values from -0.875 to 0.875
- bias_first: float32 [32], replicated, may hold values from -3 to 3
- weight_middle: bfloat16 [3, 3, 3, 32, 32], replicated, may hold values from -0.21875 to 0.21875
- bias_middle: float32 [32], replicated, may hold values from -3 to 3
- weight_last: bfloat16 [3, 3, 3, 2, 32], replicated, may hold values from -0.21875 to 0.21875
- bias_last: float32 [2], replicated, may hold values from -3 to 3
Outputs:
- solution: float32 [256, 128, 128], P(('slab', 'coil'))
- residual: float32 [256, 128, 128], P(('slab', 'coil'))
The draws below stay inside these ranges and needn't reach their ends.
All inputs are finite; a program needn't handle non-finite values. No bound on the sum of `sampling` on one device may be relied on, other than what follows from the above.
Results may differ from the reference program's by a relative error of at most 0.0018.
Values may be sent and summed in bfloat16 or wider, within the bound.
A program may use at most 128 MiB of HBM per device.

```python
import jax
import jax.numpy as jnp
from jax import lax

Y = 256
Z = 128
X = 64
CHANNELS = 32
CG_ITERS = 2
COILS = 32


def envelope_draw(key, shape_rows, shape_planes, last_size, spread):
    row_index = jnp.arange(shape_rows, dtype=jnp.float32)
    envelope = jnp.sqrt(1.0 + 5.0 * row_index / shape_rows)[:, None, None]
    values = jax.random.normal(key, (shape_rows, shape_planes, last_size))
    return values * envelope * spread


def draw_prior_image(key, part):
    values = envelope_draw(jax.random.fold_in(key, 11), Y, Z, 2 * X, 1.0)
    return jnp.clip(values, -12.0, 12.0).astype(jnp.float32)


def draw_coil_maps(key, part):
    keys = jax.random.split(jax.random.fold_in(key, 23), COILS)
    spread = 1.0 / jnp.sqrt(2.0 * COILS)
    values = jax.vmap(lambda coil_key: envelope_draw(coil_key, Y, Z, 2 * X, spread))(keys)
    return jnp.clip(values, -3.0, 3.0).astype(jnp.bfloat16)


def plant(values, own_key, least, largest):
    dims = values.shape
    place = [jax.random.randint(jax.random.fold_in(own_key, axis), (), 0, dims[axis]) for axis in range(len(dims))]
    values = values.at[tuple(place)].set(least)
    longest = dims.index(max(dims))
    place[longest] = (place[longest] + 1) % dims[longest]
    return values.at[tuple(place)].set(largest)


def steps_of(key, dims, cuts, least, high):
    level = 1.0
    for dim, blocks in cuts:
        heights = jax.random.uniform(jax.random.fold_in(jax.random.fold_in(key, 6), dim), (blocks,), jnp.float32, least / len(cuts), high / len(cuts))
        level = level * jnp.repeat(jnp.exp(heights), dims[dim] // blocks).reshape((-1,) + (1,) * (len(dims) - 1 - dim))
    return level


def scatter_about(rng, dims, scale, bound, cuts=(), kind=jnp.bfloat16):
    gain = steps_of(rng, dims, cuts, -0.22, 0.18) if cuts else 1.0
    entries = jax.random.normal(rng, dims, jnp.float32) * scale * gain
    return jnp.minimum(jnp.maximum(entries, -bound), bound).astype(kind)


def setup_inputs(seed: int = 0) -> dict:
    seeds = jax.random.split(jax.random.key(seed), 11)
    return {
        "prior_image": draw_prior_image(jax.random.fold_in(seeds[10], 71), 0),
        "coil_maps": draw_coil_maps(jax.random.fold_in(seeds[10], 71), 0),
        "kspace": scatter_about(seeds[2], (COILS, Z, Y, 2 * X), 1.0, 6.0, ((0, 32), (1, 8))),
        "sampling": plant((jax.random.randint(seeds[3], (Z, Y), 0, 3) < 1).astype(jnp.int32), jax.random.fold_in(seeds[3], 1), 0, 1),
        "weight_first": scatter_about(seeds[4], (3, 3, 3, CHANNELS, 2), 54 ** -0.5, 0.875),
        "bias_first": scatter_about(seeds[5], (CHANNELS,), 0.5, 3.0, (), jnp.float32),
        "weight_middle": scatter_about(seeds[6], (3, 3, 3, CHANNELS, CHANNELS), (27 * CHANNELS) ** -0.5, 0.21875),
        "bias_middle": scatter_about(seeds[7], (CHANNELS,), 0.5, 3.0, (), jnp.float32),
        "weight_last": scatter_about(seeds[8], (3, 3, 3, 2, CHANNELS), (27 * CHANNELS) ** -0.5, 0.21875),
        "bias_last": scatter_about(seeds[9], (2,), 0.5, 3.0, (), jnp.float32),
    }


penalty = 0.5


def convolve(features, weights, offsets):
    kernel = jnp.transpose(weights.astype(jnp.float32), (3, 4, 0, 1, 2))
    result = lax.conv_general_dilated(features.astype(jnp.float32)[None], kernel, (1, 1, 1), ((1, 1), (1, 1), (1, 1)), dimension_numbers=("NCDHW", "OIDHW", "NCDHW"), precision=lax.Precision.HIGHEST)
    return result[0] + offsets.astype(jnp.float32)[:, None, None, None]


def as_complex(volume):
    half_width = volume.shape[-1] // 2
    return lax.complex(volume[..., :half_width], volume[..., half_width:])


def as_real(volume):
    return jnp.concatenate([jnp.real(volume), jnp.imag(volume)], axis=-1)


def reference(prior_image, coil_maps, kspace, sampling, weight_first, bias_first, weight_middle, bias_middle, weight_last, bias_last):
    half_width = prior_image.shape[-1] // 2
    features = jnp.stack([prior_image[..., :half_width], prior_image[..., half_width:]]).astype(jnp.bfloat16)
    hidden = jax.nn.relu(convolve(features, weight_first, bias_first)).astype(jnp.bfloat16)
    hidden = jax.nn.relu(convolve(hidden, weight_middle, bias_middle)).astype(jnp.bfloat16)
    output = convolve(hidden, weight_last, bias_last)
    denoised = prior_image + jnp.concatenate([output[0], output[1]], axis=-1)
    sampled = jnp.transpose(sampling).astype(jnp.float32)[:, :, None]

    def adjoint_step(running, pair):
        coil_map, measured = pair
        sensitivity = as_complex(coil_map.astype(jnp.float32))
        spectrum = as_complex(jnp.transpose(measured.astype(jnp.float32), (1, 0, 2))) * sampled
        image_side = jnp.fft.ifft2(spectrum, axes=(0, 1), norm="ortho")
        return running + jnp.conj(sensitivity) * image_side, None

    adjoint = lax.scan(adjoint_step, as_complex(jnp.zeros_like(prior_image)), (coil_maps, kspace))[0]
    right_side = as_real(adjoint) + penalty * denoised

    def operator(direction):
        field_value = as_complex(direction)

        def coil_step(running, coil_map):
            sensitivity = as_complex(coil_map.astype(jnp.float32))
            spectrum = jnp.fft.fft2(sensitivity * field_value, axes=(0, 1), norm="ortho") * sampled
            image_side = jnp.fft.ifft2(spectrum, axes=(0, 1), norm="ortho")
            return running + jnp.conj(sensitivity) * image_side, None

        running = lax.scan(coil_step, as_complex(jnp.zeros_like(direction)), coil_maps)[0]
        return as_real(running) + penalty * direction

    solution = jnp.zeros_like(right_side)
    residual = right_side
    direction = right_side
    norm_now = jnp.sum(residual * residual)
    for iteration in range(CG_ITERS):
        image_dir = operator(direction)
        step_size = norm_now / jnp.sum(direction * image_dir)
        solution = solution + step_size * direction
        residual = residual - step_size * image_dir
        if iteration + 1 < CG_ITERS:
            norm_next = jnp.sum(residual * residual)
            direction = residual + (norm_next / norm_now) * direction
            norm_now = norm_next
    return solution, residual
```

```python
import functools

import jax
import jax.numpy as jnp
import numpy as np
from jax import lax
from jax.experimental import pallas as pl
from jax.experimental.pallas import tpu as pltpu
from jax.sharding import Mesh
from jax.sharding import PartitionSpec as P

AXES = ("x", "k", "y", "g", "b")
SIZES = (4, 2, 4, 4, 2)
GROUP = ("x", "k", "y", "b")
ALL = ("x", "k", "y", "g", "b")

penalty = 0.5
f32 = jnp.float32
bf16 = jnp.bfloat16


def with_halo(value, width):
    count, length = 256, value.shape[0]
    up = [(i, (i + 1) % count) for i in range(count - 1)]
    last = lax.slice_in_dim(value, length - width, length, axis=0)
    initial = lax.slice_in_dim(value, 0, width, axis=0)
    low = lax.ppermute(last, ALL, up)
    high = lax.ppermute(initial, ALL, [(b, a) for a, b in up])
    return jnp.concatenate([low, value, high], axis=0)


def convolve_layer(features, weights, offsets, readout):
    row_total = features.shape[0]
    in_channels = features.shape[1]
    span_cells = features.shape[2]
    out_channels = weights.shape[3]
    extended = with_halo(features, 1)
    padded = jnp.pad(extended, ((0, 0), (0, 0), (readout + 1, readout + 1)))
    column = (jnp.arange(padded.shape[2], dtype=jnp.int32) - 1) % readout
    zero_value = jnp.zeros((), padded.dtype)
    sources = (
        jnp.where(column != readout - 1, padded, zero_value),
        padded,
        jnp.where(column != 0, padded, zero_value),
    )
    running = jnp.zeros((row_total, out_channels, span_cells), jnp.float32)
    for row_shift in range(3):
        for plane_shift in range(3):
            pieces = []
            for column_shift in range(3):
                first_cell = plane_shift * readout + column_shift
                pieces.append(
                    lax.slice(
                        sources[column_shift],
                        (row_shift, 0, first_cell),
                        (row_shift + row_total, in_channels, first_cell + span_cells),
                    )
                )
            stacked = jnp.concatenate(pieces, axis=1)
            kernel = jnp.transpose(weights[row_shift, plane_shift], (1, 0, 2)).reshape(
                out_channels, 3 * in_channels
            )
            running = running + jnp.einsum(
                "oc,ycn->yon", kernel, stacked, preferred_element_type=jnp.float32
            )
    return running + offsets[None, :, None]


def split_table(table):
    table = table.astype(np.float32)
    high = table.astype(jnp.bfloat16)
    low = (table - high.astype(np.float32)).astype(jnp.bfloat16)
    return np.stack([high, low])


def row_order():
    order = np.zeros(256, np.int64)
    for g in range(4):
        for s in range(8):
            for y in range(4):
                for b in range(2):
                    order[g * 64 + s * 8 + y * 2 + b] = s * 32 + y * 8 + 2 * g + b
    return order


def tables():
    rows = row_order()
    angle = 2 * np.pi * (np.outer(np.arange(256), rows) % 256) / 256
    c, s = np.cos(angle) / 16.0, np.sin(angle) / 16.0
    forward = split_table(np.block([[c, s], [-s, c]]))
    backward = split_table(np.block([[c.T, -s.T], [s.T, c.T]]))
    angle = 2 * np.pi * (np.outer(np.arange(128), np.arange(128)) % 128) / 128
    c, s = np.cos(angle) / np.sqrt(128.0), np.sin(angle) / np.sqrt(128.0)
    z_forward = split_table(np.block([[c, -s], [s, c]]))
    z_backward = split_table(np.block([[c, s], [-s, c]]))
    return forward, backward, z_forward, z_backward


def halves(value):
    high = value.astype(bf16)
    low = (value - high.astype(f32)).astype(bf16)
    return high, low


def mm(a, b):
    return jnp.dot(a, b, preferred_element_type=f32)


def table_right(value, table):
    high, low = halves(value)
    return mm(high, table[0]) + (mm(high, table[1]) + mm(low, table[0]))


def table_left(table, value):
    high, low = halves(value)
    return mm(table[0], high) + (mm(table[1], high) + mm(table[0], low))


def to_rows(value):
    first, second = value[:256], value[256:]
    return jnp.concatenate(
        [
            jnp.concatenate([first[:, :128], second[:, :128]], axis=1),
            jnp.concatenate([first[:, 128:], second[:, 128:]], axis=1),
        ],
        axis=0,
    )


def to_lanes(value):
    real, imag = value[:256], value[256:]
    return jnp.concatenate(
        [
            jnp.concatenate([real[:, :128], imag[:, :128]], axis=1),
            jnp.concatenate([real[:, 128:], imag[:, 128:]], axis=1),
        ],
        axis=0,
    )


def folded(value):
    return value.reshape(-1, 8, 128).sum(axis=0)


def cg_kernel(
    den_ref,
    k_ref,
    s_ref,
    mask_ref,
    fy_ref,
    gy_ref,
    fz_ref,
    gz_ref,
    sol_ref,
    res_ref,
    acc,
    mask_all,
    mask_t,
    parts,
    own,
    full,
    stat_a,
    stat_b,
    stat_c,
    stat_own,
    send_sem,
    part_sem,
    full_sem,
    mask_sem,
    stat_sem_a,
    stat_sem_b,
    stat_sem_c,
):
    x, k, y, g, b = (lax.axis_index(name) for name in AXES)
    slab = x * 2 + k
    line = g * 2 + b

    def slab_peer(i):
        t = lax.rem(slab + i, 8)
        return t, {"x": t // 2, "k": lax.rem(t, 2)}

    def y_peer(i):
        t = lax.rem(y + i, 4)
        return t, {"y": t}

    def line_peer(i):
        t = lax.rem(line + i, 8)
        return t, {"g": t // 2, "b": lax.rem(t, 2)}

    def g_peer(i):
        t = lax.rem(g + i, 4)
        return t, {"g": t}

    barrier = pltpu.get_barrier_semaphore()
    for count, peer in ((8, slab_peer), (4, y_peer), (8, line_peer)):
        for i in range(1, count):
            pl.semaphore_signal(
                barrier, inc=1, device_id=peer(i)[1], device_id_type=pl.DeviceIdType.MESH
            )
    pl.semaphore_wait(barrier, 17)

    def send(source, target, slot, arrival, device):
        copy = pltpu.make_async_remote_copy(
            src_ref=source,
            dst_ref=target,
            send_sem=send_sem.at[slot],
            recv_sem=arrival,
            device_id=device,
            device_id_type=pl.DeviceIdType.MESH,
        )
        copy.start()
        return copy

    mask_copies = []
    for i in range(1, 8):
        mask_copies.append(
            send(mask_ref, mask_all.at[slab], i - 1, mask_sem.at[i - 1], slab_peer(i)[1])
        )
    mask_all[pl.ds(slab, 1)] = mask_ref[...][None]

    acc[...] = jnp.zeros_like(acc)

    def maps_of(j):
        return s_ref[j, 0].astype(f32), s_ref[j, 1].astype(f32)

    def add_image(image, pair):
        for n in range(2):
            real, imag = maps_of(2 * pair + n)
            a_real = image[256 * n : 256 * n + 256, :128]
            a_imag = image[256 * n : 256 * n + 256, 128:]
            acc[0] += real * a_real + imag * a_imag
            acc[1] += real * a_imag - imag * a_real

    def adjoint_pair(pair, _):
        planes = []
        for n in range(2):
            j = 2 * pair + n
            planes.append(
                jnp.concatenate(
                    [k_ref[:, j, 0].reshape(128, 256), k_ref[:, j, 1].reshape(128, 256)], axis=1
                )
            )
        spectrum = jnp.concatenate(planes, axis=0)
        dims = (((1,), (1,)), ((), ()))
        rows = lax.dot_general(
            gy_ref[0], spectrum, dims, preferred_element_type=f32
        ) + lax.dot_general(gy_ref[1], spectrum, dims, preferred_element_type=f32)
        add_image(table_right(to_lanes(rows), gz_ref), pair)
        return 0

    lax.fori_loop(0, 4, adjoint_pair, 0)

    def reduce_scatter(step):
        copies = []
        for i in range(1, 4):
            t, device = g_peer(i)
            first = pl.multiple_of(t * 64, 64)
            copies.append(
                send(
                    acc.at[:, pl.ds(first, 64)],
                    parts.at[step, i - 1],
                    14 + i,
                    part_sem.at[step, i - 1],
                    device,
                )
            )
        mine = acc[:, pl.ds(pl.multiple_of(g * 64, 64), 64)]

        def finish():
            for copy in copies:
                copy.wait()
            return mine + ((parts[step, 0] + parts[step, 1]) + parts[step, 2])

        return finish

    def gather(step, value):
        mine = pl.ds(pl.multiple_of(g * 64, 64), 64)
        own[step] = value
        full[step, :, mine] = value
        copies = []
        for i in range(1, 4):
            _, device = g_peer(i)
            copies.append(
                send(
                    own.at[step],
                    full.at[step, :, mine],
                    14 + i,
                    full_sem.at[step, i - 1],
                    device,
                )
            )
        return copies

    right = reduce_scatter(0)() + penalty * den_ref[...]
    gathers = gather(0, right)
    for copy in mask_copies:
        copy.wait_recv()
    eye = (
        lax.broadcasted_iota(jnp.int32, (256, 256), 0)
        == lax.broadcasted_iota(jnp.int32, (256, 256), 1)
    ).astype(bf16)
    mask_t[...] = lax.dot_general(
        eye, mask_all[...].reshape(128, 256), (((1,), (1,)), ((), ())), preferred_element_type=f32
    )

    def operator(step):
        acc[...] = jnp.zeros_like(acc)

        def one_pair(pair, energy):
            d_real, d_imag = full[step, 0], full[step, 1]
            pieces = []
            for n in range(2):
                real, imag = maps_of(2 * pair + n)
                pieces.append(
                    jnp.concatenate(
                        [real * d_real - imag * d_imag, real * d_imag + imag * d_real], axis=1
                    )
                )
            spectrum = to_rows(table_right(jnp.concatenate(pieces, axis=0), fz_ref))
            mask = mask_t[...]
            mask = jnp.concatenate([mask, mask], axis=1)
            mask = jnp.concatenate([mask, mask], axis=0)
            spectrum = table_left(fy_ref, spectrum) * mask
            squares = spectrum * spectrum
            energy = energy + folded(squares[:, :128] + squares[:, 128:])
            image = to_lanes(table_left(gy_ref, spectrum))
            add_image(table_right(image, gz_ref), pair)
            return energy

        return lax.fori_loop(0, 4, one_pair, jnp.zeros((8, 128), f32))

    def totals(step, norm, energy):
        value = jnp.stack([norm, energy])
        stages = (
            (8, slab_peer, slab, stat_a, stat_sem_a),
            (4, y_peer, y, stat_b, stat_sem_b),
            (8, line_peer, line, stat_c, stat_sem_c),
        )
        for stage, (count, peer, me, slots, sems) in enumerate(stages):
            stat_own[step, stage] = value
            slots[step, pl.ds(me, 1)] = value[None]
            copies = []
            for i in range(1, count):
                copies.append(
                    send(
                        stat_own.at[step, stage],
                        slots.at[step, me],
                        7 + i,
                        sems.at[step, i - 1],
                        peer(i)[1],
                    )
                )
            for copy in copies:
                copy.wait()
            value = slots[step, 0]
            for i in range(1, count):
                value = value + slots[step, i]
        return jnp.sum(value[0]), jnp.sum(value[1])

    def norm_of(value):
        return folded((value * value).reshape(128, 128))

    for copy in mask_copies:
        copy.wait_send()

    for copy in gathers:
        copy.wait()
    energy = operator(0)
    finish = reduce_scatter(1)
    rr, energy = totals(0, norm_of(right), energy)
    alpha = rr / (energy + penalty * rr)
    image = finish() + penalty * right
    residual = right - alpha * image
    gathers = gather(1, residual)
    for copy in gathers:
        copy.wait()
    energy = operator(1)
    finish = reduce_scatter(2)
    fresh, energy = totals(1, norm_of(residual), energy)
    growth = fresh / rr
    step_size = fresh / (energy + penalty * fresh - growth * fresh / alpha)
    q = finish() + penalty * residual + growth * image
    sol_ref[...] = alpha * right + step_size * (residual + growth * right)
    res_ref[...] = residual - step_size * q


def cg(den, spectrum, maps, mask):
    forward, backward, z_forward, z_backward = tables()
    vmem = pl.BlockSpec(memory_space=pltpu.VMEM)
    out = jax.ShapeDtypeStruct((2, 64, 128), f32)
    dma = pltpu.SemaphoreType.DMA
    return pl.pallas_call(
        cg_kernel,
        out_shape=(out, out),
        in_specs=[vmem] * 8,
        out_specs=(vmem, vmem),
        scratch_shapes=[
            pltpu.VMEM((2, 256, 128), f32),
            pltpu.VMEM((8, 16, 256), bf16),
            pltpu.VMEM((256, 128), f32),
            pltpu.VMEM((3, 3, 2, 64, 128), f32),
            pltpu.VMEM((2, 2, 64, 128), f32),
            pltpu.VMEM((2, 2, 256, 128), f32),
            pltpu.VMEM((2, 8, 2, 8, 128), f32),
            pltpu.VMEM((2, 4, 2, 8, 128), f32),
            pltpu.VMEM((2, 8, 2, 8, 128), f32),
            pltpu.VMEM((2, 3, 2, 8, 128), f32),
            dma((18,)),
            dma((3, 3)),
            dma((2, 3)),
            dma((7,)),
            dma((2, 7)),
            dma((2, 3)),
            dma((2, 7)),
        ],
        compiler_params=pltpu.CompilerParams(
            collective_id=0, has_side_effects=True, vmem_limit_bytes=60 * 1024 * 1024
        ),
    )(
        den,
        spectrum,
        maps,
        mask,
        jnp.asarray(forward),
        jnp.asarray(backward),
        jnp.asarray(z_forward),
        jnp.asarray(z_backward),
    )


def body(
    prior_image,
    coil_maps,
    kspace,
    sampling,
    weight_first,
    bias_first,
    weight_middle,
    bias_middle,
    weight_last,
    bias_last,
):
    readout = prior_image.shape[2] // 2
    own_rows = prior_image.shape[0]
    planes = prior_image.shape[1]

    def exchange(value):
        return lax.all_to_all(value, GROUP, split_axis=0, concat_axis=0, tiled=True)

    mask = sampling.astype(bf16)
    measured = kspace[0] * mask[:, :, None]
    spectrum = exchange(measured.reshape(16, 256, 2, 64).transpose(3, 2, 0, 1))
    spectrum = spectrum.reshape(8, 8, 2, 16, 256)
    maps = coil_maps[0].reshape(4, 4, 2, 128, 2, 64).transpose(5, 4, 1, 0, 2, 3)
    maps = exchange(maps.reshape(64, 2, 4, 8, 128))
    maps = maps.reshape(8, 8, 2, 4, 8, 128).transpose(1, 2, 3, 0, 4, 5).reshape(8, 2, 256, 128)

    features = (
        jnp.stack([prior_image[..., :readout], prior_image[..., readout:]], axis=1)
        .reshape(own_rows, 2, planes * readout)
        .astype(jnp.bfloat16)
    )
    hidden = jax.nn.relu(convolve_layer(features, weight_first, bias_first, readout)).astype(
        jnp.bfloat16
    )
    hidden = jax.nn.relu(convolve_layer(hidden, weight_middle, bias_middle, readout)).astype(
        jnp.bfloat16
    )
    output = convolve_layer(hidden, weight_last, bias_last, readout).reshape(
        own_rows, 2, planes, readout
    )
    denoised = prior_image + jnp.concatenate([output[:, 0], output[:, 1]], axis=-1)
    den = exchange(denoised[0].reshape(128, 2, 64).transpose(2, 1, 0)).transpose(1, 0, 2)
    sol, res = cg(den, spectrum, maps, mask)
    both = exchange(jnp.stack([sol, res]).transpose(2, 0, 1, 3))
    both = both.transpose(1, 3, 2, 0).reshape(2, 1, 128, 128)
    return both[0], both[1]


def solution(mesh):
    torus = Mesh(mesh.devices.reshape(SIZES), AXES)
    coil = ("y", "g", "b")
    slab = ("x", "k")
    in_specs = (
        P(ALL, None, None),
        P(coil, slab, None, None),
        P(coil, slab, None, None),
        P(slab, None),
        P(),
        P(),
        P(),
        P(),
        P(),
        P(),
    )
    out_specs = (P(ALL, None, None), P(ALL, None, None))
    return jax.shard_map(body, mesh=torus, in_specs=in_specs, out_specs=out_specs, check_vma=False)
```

```python
import functools

import jax
import jax.numpy as jnp
import numpy as np
from jax import lax
from jax.experimental import pallas as pl
from jax.experimental.pallas import tpu as pltpu
from jax.sharding import Mesh
from jax.sharding import PartitionSpec as P

AXES = ("x", "k", "y", "g", "b")
SIZES = (4, 2, 4, 4, 2)
GROUP = ("x", "k", "y", "b")
ALL = ("x", "k", "y", "g", "b")

penalty = 0.5
f32 = jnp.float32
bf16 = jnp.bfloat16


def split_table(table):
    table = table.astype(np.float32)
    high = table.astype(jnp.bfloat16)
    low = (table - high.astype(np.float32)).astype(jnp.bfloat16)
    return np.stack([high, low])


def row_order():
    order = np.zeros(256, np.int64)
    for g in range(4):
        for s in range(8):
            for y in range(4):
                for b in range(2):
                    order[g * 64 + s * 8 + y * 2 + b] = s * 32 + y * 8 + 2 * g + b
    return order


def tables():
    rows = row_order()
    angle = 2 * np.pi * (np.outer(np.arange(256), rows) % 256) / 256
    c, s = np.cos(angle) / 16.0, np.sin(angle) / 16.0
    forward = split_table(np.block([[c, s], [-s, c]]))
    backward = split_table(np.block([[c.T, -s.T], [s.T, c.T]]))
    angle = 2 * np.pi * (np.outer(np.arange(128), np.arange(128)) % 128) / 128
    c, s = np.cos(angle) / np.sqrt(128.0), np.sin(angle) / np.sqrt(128.0)
    z_forward = split_table(np.block([[c, -s], [s, c]]))
    z_backward = split_table(np.block([[c, s], [-s, c]]))
    return forward, backward, z_forward, z_backward


def halves(value):
    high = value.astype(bf16)
    low = (value - high.astype(f32)).astype(bf16)
    return high, low


def mm(a, b):
    return jnp.dot(a, b, preferred_element_type=f32)


def table_right(value, table):
    high, low = halves(value)
    return mm(high, table[0]) + (mm(high, table[1]) + mm(low, table[0]))


def table_left(table, value):
    high, low = halves(value)
    return mm(table[0], high) + (mm(table[1], high) + mm(table[0], low))


def to_rows(value):
    first, second = value[:256], value[256:]
    return jnp.concatenate(
        [
            jnp.concatenate([first[:, :128], second[:, :128]], axis=1),
            jnp.concatenate([first[:, 128:], second[:, 128:]], axis=1),
        ],
        axis=0,
    )


def to_lanes(value):
    real, imag = value[:256], value[256:]
    return jnp.concatenate(
        [
            jnp.concatenate([real[:, :128], imag[:, :128]], axis=1),
            jnp.concatenate([real[:, 128:], imag[:, 128:]], axis=1),
        ],
        axis=0,
    )


def folded(value):
    return value.reshape(-1, 8, 128).sum(axis=0)


def decode_group(i):
    return {"x": i // 16, "k": lax.rem(i // 8, 2), "y": lax.rem(i // 2, 4), "b": lax.rem(i, 2)}


def decode_all(i):
    return {
        "x": i // 64,
        "k": lax.rem(i // 32, 2),
        "y": lax.rem(i // 8, 4),
        "g": lax.rem(i // 2, 4),
        "b": lax.rem(i, 2),
    }


def lanes(shape):
    return lax.broadcasted_iota(jnp.int32, shape, len(shape) - 1)


def plane_shift(value, dz):
    if dz == 0:
        return value
    if dz < 0:
        edge = pltpu.roll(value[:, -128:], 64, 1)
        edge = jnp.where(lanes(edge.shape) >= 64, edge, 0.0)
        return jnp.concatenate([edge, value[:, :-128]], axis=1)
    edge = pltpu.roll(value[:, :128], 64, 1)
    edge = jnp.where(lanes(edge.shape) < 64, edge, 0.0)
    return jnp.concatenate([value[:, 128:], edge], axis=1)


def column_shift(value, dx):
    if dx == 0:
        return value
    width = value.shape[1]
    column = lax.rem(lanes(value.shape), 64)
    if dx < 0:
        return jnp.where(column != 0, pltpu.roll(value, 1, 1), 0.0)
    return jnp.where(column != 63, pltpu.roll(value, width - 1, 1), 0.0)


def step_kernel(
    feat_ref,
    prior_ref,
    k_hbm,
    m_hbm,
    mask_ref,
    w1_ref,
    w2_ref,
    w3_ref,
    b1_ref,
    b2_ref,
    b3_ref,
    fy_ref,
    gy_ref,
    fz_ref,
    gz_ref,
    sol_ref,
    res_ref,
    k_ref,
    m_ref,
    s_ref,
    fbuf,
    f_rows,
    a1,
    h1m,
    h1e,
    p3,
    dplanes,
    dsrc,
    dbuf,
    osrc,
    obuf,
    acc,
    mask_all,
    mask_t,
    parts,
    own,
    full,
    stat_a,
    stat_b,
    stat_c,
    stat_own,
    send_sem,
    part_sem,
    full_sem,
    mask_sem,
    stat_sem_a,
    stat_sem_b,
    stat_sem_c,
    feat_send,
    feat_sem,
    bulk_send,
    bulk_sem,
    local_sem,
):
    x, k, y, g, b = (lax.axis_index(name) for name in AXES)
    slab = x * 2 + k
    line = g * 2 + b
    me = x * 16 + k * 8 + y * 2 + b
    row = slab * 32 + y * 8 + line

    def group_peer(i):
        t = lax.rem(me + i, 64)
        return t, decode_group(t)

    def row_peer(i):
        return decode_all(lax.rem(row + 256 + i, 256))

    def slab_peer(i):
        t = lax.rem(slab + i, 8)
        return t, {"x": t // 2, "k": lax.rem(t, 2)}

    def y_peer(i):
        t = lax.rem(y + i, 4)
        return t, {"y": t}

    def line_peer(i):
        t = lax.rem(line + i, 8)
        return t, {"g": t // 2, "b": lax.rem(t, 2)}

    def g_peer(i):
        t = lax.rem(g + i, 4)
        return t, {"g": t}

    mesh_id = pl.DeviceIdType.MESH
    barrier = pltpu.get_barrier_semaphore()

    def greet(i, _):
        pl.semaphore_signal(barrier, inc=1, device_id=group_peer(i)[1], device_id_type=mesh_id)
        return 0

    for i in (-3, -2, -1, 1, 2, 3):
        pl.semaphore_signal(barrier, inc=1, device_id=row_peer(i), device_id_type=mesh_id)
    for i in range(1, 4):
        for c in range(2):
            pl.semaphore_signal(
                barrier,
                inc=1,
                device_id={"g": lax.rem(g + i, 4), "b": lax.rem(b + c, 2)},
                device_id_type=mesh_id,
            )
    lax.fori_loop(1, 64, greet, 0)
    k_local = pltpu.make_async_copy(k_hbm.at[me], k_ref.at[me], local_sem.at[0])
    m_local = pltpu.make_async_copy(m_hbm.at[me], m_ref.at[me], local_sem.at[1])
    k_local.start()
    m_local.start()
    pl.semaphore_wait(barrier, 75)

    def copy_to(source, target, departure, arrival, device):
        copy = pltpu.make_async_remote_copy(
            src_ref=source,
            dst_ref=target,
            send_sem=departure,
            recv_sem=arrival,
            device_id=device,
            device_id_type=mesh_id,
        )
        copy.start()
        return copy

    def send(source, target, slot, arrival, device):
        return copy_to(source, target, send_sem.at[slot], arrival, device)

    def bulk(which, source, target):
        def one(i, _):
            t, device = group_peer(i)
            copy_to(source.at[t], target.at[me], bulk_send.at[which], bulk_sem.at[which], device)
            return 0

        lax.fori_loop(1, 64, one, 0)

    def bulk_wait(which, source, target):
        pltpu.make_async_copy(
            target.at[pl.ds(0, 63)], target.at[pl.ds(0, 63)], bulk_sem.at[which]
        ).wait()
        pltpu.make_async_copy(
            source.at[pl.ds(0, 63)], source.at[pl.ds(0, 63)], bulk_send.at[which]
        ).wait()

    feat_copies = []
    for n, i in enumerate((-1, 1, -2, 2, -3, 3)):
        feat_copies.append(
            copy_to(feat_ref, fbuf.at[3 - i], feat_send.at[n], feat_sem.at[n], row_peer(i))
        )
    bulk(0, k_hbm, k_ref)
    mask_copies = []
    for i in range(1, 8):
        mask_copies.append(
            send(mask_ref, mask_all.at[slab], i - 1, mask_sem.at[i - 1], slab_peer(i)[1])
        )
    mask_all[pl.ds(slab, 1)] = mask_ref[...][None]
    bulk(1, m_hbm, m_ref)

    fbuf[3] = feat_ref[...]
    for copy in feat_copies:
        copy.wait()
    f_rows[14:16] = jnp.zeros((2, 8192), f32)
    for r in range(7):
        inside = jnp.logical_and(row + r >= 3, row + r < 259)
        f_rows[2 * r : 2 * r + 2] = jnp.where(inside, fbuf[r].astype(f32), 0.0)
    for dx in range(3):
        shifted = column_shift(f_rows[...], dx - 1)
        for dz in range(3):
            tap = dz * 3 + dx
            a1[16 * tap : 16 * tap + 16] = plane_shift(shifted, dz - 1).astype(bf16)

    lane = lanes((1, 256))
    hidden_row = row - 2 + jnp.minimum(lane // 32, 4)
    keep1 = jnp.where(jnp.logical_and(hidden_row >= 0, hidden_row < 256), 1.0, 0.0)
    lane = lanes((1, 128))
    hidden_row = row - 1 + jnp.minimum(lane // 32, 2)
    keep2 = jnp.where(jnp.logical_and(hidden_row >= 0, hidden_row < 256), 1.0, 0.0)
    h1e[...] = jnp.zeros_like(h1e)

    def layer_one(n, _):
        first = pl.multiple_of(n * 512, 512)
        block = lax.dot_general(
            a1[:, pl.ds(first, 512)],
            w1_ref[...],
            (((0,), (0,)), ((), ())),
            preferred_element_type=f32,
        )
        block = (jnp.maximum(block + b1_ref[...], 0.0) * keep1).astype(bf16)
        h1m[pl.ds(pl.multiple_of(first + 128, 128), 512)] = block[:, :128]
        for dz in range(3):
            h1e[pl.ds(pl.multiple_of(first + 256 - 128 * dz, 128), 512), 32 * dz : 32 * dz + 32] = (
                block[:, 128 + 32 * dz : 160 + 32 * dz]
            )
        return 0

    lax.fori_loop(0, 16, layer_one, 0)
    zero = jnp.zeros((64, 128), bf16)
    h1m[0:64] = zero
    h1m[64:128] = h1m[128 + 8064 : 128 + 8128]
    h1m[128 + 8192 : 128 + 8256] = h1m[192:256]
    h1m[128 + 8256 : 128 + 8320] = zero
    h1e[128:192, 0:32] = jnp.zeros((64, 32), bf16)
    h1e[192:256, 0:32] = h1e[128 + 8064 : 128 + 8128, 32:64]
    return_rows = h1e[192:256, 32:64]
    h1e[128 + 8064 : 128 + 8128, 64:96] = return_rows
    h1e[128 + 8128 : 128 + 8192, 64:96] = jnp.zeros((64, 32), bf16)

    def layer_two(n, _):
        first = pl.multiple_of(n * 512, 512)
        low = jnp.concatenate(
            [
                h1m[pl.ds(first, 512)],
                h1m[pl.ds(pl.multiple_of(first + 128, 128), 512)],
                h1m[pl.ds(pl.multiple_of(first + 256, 128), 512)],
                h1e[pl.ds(pl.multiple_of(first + 128, 128), 512)],
            ],
            axis=1,
        )
        block = mm(low, w2_ref[...])
        column = lax.rem(lax.broadcasted_iota(jnp.int32, (512, 128), 0), 64)
        block = (
            jnp.where(column != 0, pltpu.roll(block[:, :128], 1, 0), 0.0)
            + block[:, 128:256]
            + jnp.where(column != 63, pltpu.roll(block[:, 256:], 511, 0), 0.0)
        )
        block = (jnp.maximum(block + b2_ref[...], 0.0) * keep2).astype(bf16)
        p3[:, pl.ds(first, 512)] = lax.dot_general(
            w3_ref[...], block, (((1,), (1,)), ((), ())), preferred_element_type=f32
        )
        return 0

    lax.fori_loop(0, 16, layer_two, 0)
    total = jnp.zeros((8, 8192), f32)
    for dx in range(3):
        side = jnp.zeros((8, 8192), f32)
        for dz in range(3):
            tap = dz * 3 + dx
            side = side + plane_shift(p3[8 * tap : 8 * tap + 8], dz - 1)
        total = total + column_shift(side, dx - 1)
    total = total[0:2] + (prior_ref[...] + b3_ref[...])
    for i in range(64):
        for c in range(2):
            dplanes[c, i : i + 1] = total[c : c + 1, 128 * i : 128 * i + 128]
    for c in range(2):
        turned = jnp.transpose(dplanes[c])
        dsrc[:, c] = jnp.concatenate([turned[:64], turned[64:]], axis=1)
    bulk(2, dsrc, dbuf)
    dbuf[pl.ds(me, 1)] = dsrc[pl.ds(me, 1)]

    acc[...] = jnp.zeros_like(acc)

    def maps_of(j):
        return s_ref[j, 0], s_ref[j, 1]

    def add_image(image, pair):
        for n in range(2):
            real, imag = maps_of(2 * pair + n)
            a_real = image[256 * n : 256 * n + 256, :128]
            a_imag = image[256 * n : 256 * n + 256, 128:]
            acc[0] += real * a_real + imag * a_imag
            acc[1] += real * a_imag - imag * a_real

    k_local.wait()
    m_local.wait()
    bulk_wait(0, k_hbm, k_ref)
    bulk_wait(1, m_hbm, m_ref)

    def adjoint_pair(pair, _):
        planes = []
        for n in range(2):
            j = 2 * pair + n
            planes.append(
                jnp.concatenate(
                    [
                        jnp.concatenate([k_ref[8 * s + j, c] for s in range(8)], axis=0)
                        for c in range(2)
                    ],
                    axis=1,
                )
            )
            for c in range(2):
                for h in range(4):
                    for s in range(8):
                        first = h * 64 + s * 8
                        s_ref[j, c, first : first + 8] = m_ref[8 * s + j, c, h].astype(f32)
        spectrum = jnp.concatenate(planes, axis=0)
        dims = (((1,), (1,)), ((), ()))
        rows = lax.dot_general(
            gy_ref[0], spectrum, dims, preferred_element_type=f32
        ) + lax.dot_general(gy_ref[1], spectrum, dims, preferred_element_type=f32)
        add_image(table_right(to_lanes(rows), gz_ref), pair)
        return 0

    lax.fori_loop(0, 4, adjoint_pair, 0)

    def reduce_scatter(step):
        copies = []
        for i in range(1, 4):
            t, device = g_peer(i)
            first = pl.multiple_of(t * 64, 64)
            copies.append(
                send(
                    acc.at[:, pl.ds(first, 64)],
                    parts.at[step, i - 1],
                    14 + i,
                    part_sem.at[step, i - 1],
                    device,
                )
            )
        mine = acc[:, pl.ds(pl.multiple_of(g * 64, 64), 64)]

        def finish():
            for copy in copies:
                copy.wait()
            return mine + ((parts[step, 0] + parts[step, 1]) + parts[step, 2])

        return finish

    def gather(step, value):
        mine = pl.ds(pl.multiple_of(g * 64, 64), 64)
        own[step] = value
        full[step, :, mine] = value
        copies = []
        for i in range(1, 4):
            _, device = g_peer(i)
            copies.append(
                send(
                    own.at[step],
                    full.at[step, :, mine],
                    14 + i,
                    full_sem.at[step, i - 1],
                    device,
                )
            )
        return copies

    right = reduce_scatter(0)()
    bulk_wait(2, dsrc, dbuf)
    right = right + penalty * jnp.stack([dbuf[:, 0], dbuf[:, 1]])
    gathers = gather(0, right)
    for copy in mask_copies:
        copy.wait_recv()
    eye = (
        lax.broadcasted_iota(jnp.int32, (256, 256), 0)
        == lax.broadcasted_iota(jnp.int32, (256, 256), 1)
    ).astype(bf16)
    mask_t[...] = lax.dot_general(
        eye, mask_all[...].reshape(128, 256), (((1,), (1,)), ((), ())), preferred_element_type=f32
    )

    def operator(step):
        acc[...] = jnp.zeros_like(acc)

        def one_pair(pair, energy):
            d_real, d_imag = full[step, 0], full[step, 1]
            pieces = []
            for n in range(2):
                real, imag = maps_of(2 * pair + n)
                pieces.append(
                    jnp.concatenate(
                        [real * d_real - imag * d_imag, real * d_imag + imag * d_real], axis=1
                    )
                )
            spectrum = to_rows(table_right(jnp.concatenate(pieces, axis=0), fz_ref))
            mask = mask_t[...]
            mask = jnp.concatenate([mask, mask], axis=1)
            mask = jnp.concatenate([mask, mask], axis=0)
            spectrum = table_left(fy_ref, spectrum) * mask
            squares = spectrum * spectrum
            energy = energy + folded(squares[:, :128] + squares[:, 128:])
            image = to_lanes(table_left(gy_ref, spectrum))
            add_image(table_right(image, gz_ref), pair)
            return energy

        return lax.fori_loop(0, 4, one_pair, jnp.zeros((8, 128), f32))

    def totals(step, norm, energy):
        value = jnp.stack([norm, energy])
        stages = (
            (8, slab_peer, slab, stat_a, stat_sem_a),
            (4, y_peer, y, stat_b, stat_sem_b),
            (8, line_peer, line, stat_c, stat_sem_c),
        )
        for stage, (count, peer, me, slots, sems) in enumerate(stages):
            stat_own[step, stage] = value
            slots[step, pl.ds(me, 1)] = value[None]
            copies = []
            for i in range(1, count):
                copies.append(
                    send(
                        stat_own.at[step, stage],
                        slots.at[step, me],
                        7 + i,
                        sems.at[step, i - 1],
                        peer(i)[1],
                    )
                )
            for copy in copies:
                copy.wait()
            value = slots[step, 0]
            for i in range(1, count):
                value = value + slots[step, i]
        return jnp.sum(value[0]), jnp.sum(value[1])

    def norm_of(value):
        return folded((value * value).reshape(128, 128))

    for copy in mask_copies:
        copy.wait_send()

    for copy in gathers:
        copy.wait()
    energy = operator(0)
    finish = reduce_scatter(1)
    rr, energy = totals(0, norm_of(right), energy)
    alpha = rr / (energy + penalty * rr)
    image = finish() + penalty * right
    residual = right - alpha * image
    gathers = gather(1, residual)
    for copy in gathers:
        copy.wait()
    energy = operator(1)
    finish = reduce_scatter(2)
    fresh, energy = totals(1, norm_of(residual), energy)
    growth = fresh / rr
    step_size = fresh / (energy + penalty * fresh - growth * fresh / alpha)
    q = finish() + penalty * residual + growth * image
    answer = alpha * right + step_size * (residual + growth * right)
    rest = residual - step_size * q
    for c in range(2):
        osrc[:, c] = answer[c]
        osrc[:, 2 + c] = rest[c]
    bulk(3, osrc, obuf)
    obuf[pl.ds(me, 1)] = osrc[pl.ds(me, 1)]
    bulk_wait(3, osrc, obuf)
    sol_ref[...] = jnp.transpose(jnp.concatenate([obuf[:, 0], obuf[:, 1]], axis=0))
    res_ref[...] = jnp.transpose(jnp.concatenate([obuf[:, 2], obuf[:, 3]], axis=0))


def body(
    prior_image,
    coil_maps,
    kspace,
    sampling,
    weight_first,
    bias_first,
    weight_middle,
    bias_middle,
    weight_last,
    bias_last,
):
    mask = sampling.astype(bf16)
    measured = kspace[0] * mask[:, :, None]
    spectrum = measured.reshape(16, 256, 2, 64).transpose(3, 2, 0, 1)
    maps = coil_maps[0].reshape(4, 4, 2, 128, 2, 64).transpose(5, 4, 1, 0, 2, 3)
    maps = maps.reshape(64, 2, 4, 8, 128)
    prior = prior_image.reshape(2, 64, 2, 64).transpose(2, 1, 0, 3).reshape(2, 8192)
    features = prior.astype(bf16)

    first = weight_first.transpose(1, 2, 0, 4, 3).reshape(9, 6, 32)
    pieces = [jnp.pad(first, ((0, 0), (2 * r, 10 - 2 * r), (0, 0))) for r in (0, 1, 2, 3, 4, 4, 4)]
    w1 = jnp.pad(jnp.concatenate(pieces, axis=2), ((0, 0), (0, 0), (0, 32))).reshape(144, 256)
    middle = weight_middle.transpose(1, 0, 4, 2, 3).reshape(3, 96, 3, 32)
    pieces = [jnp.pad(middle, ((0, 0), (32 * r, 64 - 32 * r), (0, 0), (0, 0))) for r in range(3)]
    middle = jnp.concatenate(pieces + [jnp.zeros_like(pieces[0])], axis=3).reshape(3, 160, 384)
    w2 = jnp.concatenate(
        [
            middle[:, :128].reshape(384, 384),
            middle[:, 128:].reshape(96, 384),
            jnp.zeros((32, 384), bf16),
        ],
        axis=0,
    )
    w3 = weight_last.transpose(1, 2, 3, 0, 4).reshape(9, 2, 96)
    w3 = jnp.pad(w3, ((0, 0), (0, 6), (0, 32))).reshape(72, 128)
    b1 = jnp.tile(bias_first, 8)[None]
    b2 = jnp.tile(bias_middle, 4)[None]
    b3 = bias_last[:, None]

    forward, backward, z_forward, z_backward = tables()
    vmem = pl.BlockSpec(memory_space=pltpu.VMEM)
    hbm = pl.BlockSpec(memory_space=pl.ANY)
    out = jax.ShapeDtypeStruct((128, 128), f32)
    dma = pltpu.SemaphoreType.DMA
    sol, res = pl.pallas_call(
        step_kernel,
        out_shape=(out, out),
        in_specs=[vmem] * 2 + [hbm] * 2 + [vmem] * 11,
        out_specs=(vmem, vmem),
        scratch_shapes=[
            pltpu.VMEM((64, 2, 16, 256), bf16),
            pltpu.VMEM((64, 2, 4, 8, 128), bf16),
            pltpu.VMEM((8, 2, 256, 128), f32),
            pltpu.VMEM((7, 2, 8192), bf16),
            pltpu.VMEM((16, 8192), f32),
            pltpu.VMEM((144, 8192), bf16),
            pltpu.VMEM((8448, 128), bf16),
            pltpu.VMEM((8448, 128), bf16),
            pltpu.VMEM((72, 8192), f32),
            pltpu.VMEM((2, 64, 128), f32),
            pltpu.VMEM((64, 2, 128), f32),
            pltpu.VMEM((64, 2, 128), f32),
            pltpu.VMEM((64, 4, 128), f32),
            pltpu.VMEM((64, 4, 128), f32),
            pltpu.VMEM((2, 256, 128), f32),
            pltpu.VMEM((8, 16, 256), bf16),
            pltpu.VMEM((256, 128), f32),
            pltpu.VMEM((3, 3, 2, 64, 128), f32),
            pltpu.VMEM((2, 2, 64, 128), f32),
            pltpu.VMEM((2, 2, 256, 128), f32),
            pltpu.VMEM((2, 8, 2, 8, 128), f32),
            pltpu.VMEM((2, 4, 2, 8, 128), f32),
            pltpu.VMEM((2, 8, 2, 8, 128), f32),
            pltpu.VMEM((2, 3, 2, 8, 128), f32),
            dma((18,)),
            dma((3, 3)),
            dma((2, 3)),
            dma((7,)),
            dma((2, 7)),
            dma((2, 3)),
            dma((2, 7)),
            dma((6,)),
            dma((6,)),
            dma((4,)),
            dma((4,)),
            dma((2,)),
        ],
        compiler_params=pltpu.CompilerParams(
            collective_id=0, has_side_effects=True, vmem_limit_bytes=60 * 1024 * 1024
        ),
    )(
        features,
        prior,
        spectrum,
        maps,
        mask,
        w1,
        w2,
        w3,
        b1,
        b2,
        b3,
        jnp.asarray(forward),
        jnp.asarray(backward),
        jnp.asarray(z_forward),
        jnp.asarray(z_backward),
    )
    return sol[None], res[None]


def solution(mesh):
    torus = Mesh(mesh.devices.reshape(SIZES), AXES)
    coil = ("y", "g", "b")
    slab = ("x", "k")
    in_specs = (
        P(ALL, None, None),
        P(coil, slab, None, None),
        P(coil, slab, None, None),
        P(slab, None),
        P(),
        P(),
        P(),
        P(),
        P(),
        P(),
    )
    out_specs = (P(ALL, None, None), P(ALL, None, None))
    return jax.shard_map(body, mesh=torus, in_specs=in_specs, out_specs=out_specs, check_vma=False)
```

```python
import functools

import jax
import jax.numpy as jnp
import numpy as np
from jax import lax
from jax.experimental import pallas as pl
from jax.experimental.pallas import tpu as pltpu
from jax.sharding import Mesh
from jax.sharding import PartitionSpec as P

AXES = ("x", "k", "y", "g", "b")
SIZES = (4, 2, 4, 4, 2)
GROUP = ("x", "k", "y", "b")
ALL = ("x", "k", "y", "g", "b")

penalty = 0.5
f32 = jnp.float32
bf16 = jnp.bfloat16


def split_table(table):
    table = table.astype(np.float32)
    high = table.astype(jnp.bfloat16)
    low = (table - high.astype(np.float32)).astype(jnp.bfloat16)
    return np.stack([high, low])


def row_order():
    order = np.zeros(256, np.int64)
    for g in range(4):
        for s in range(8):
            for y in range(4):
                for b in range(2):
                    order[g * 64 + s * 8 + y * 2 + b] = s * 32 + y * 8 + 2 * g + b
    return order


def tables():
    rows = row_order().reshape(4, 2, 32)[:, 0].reshape(128)
    forward, backward = [], []
    for parity in range(2):
        angle = 2 * np.pi * (np.outer(2 * np.arange(128) + parity, rows) % 256) / 256
        c, s = np.cos(angle) / 16.0, np.sin(angle) / 16.0
        forward.append(split_table(np.block([[c, s], [-s, c]])))
        backward.append(split_table(np.block([[c.T, -s.T], [s.T, c.T]])))
    angle = 2 * np.pi * (np.outer(np.arange(128), np.arange(128)) % 128) / 128
    c, s = np.cos(angle) / np.sqrt(128.0), np.sin(angle) / np.sqrt(128.0)
    z_forward = split_table(np.block([[c, -s], [s, c]]))
    z_backward = split_table(np.block([[c, s], [-s, c]]))
    return np.stack(forward), np.stack(backward), z_forward, z_backward


def halves(value):
    high = value.astype(bf16)
    low = (value - high.astype(f32)).astype(bf16)
    return high, low


def mm(a, b):
    return jnp.dot(a, b, preferred_element_type=f32)


def table_right(value, table):
    high, low = halves(value)
    return mm(high, table[0]) + (mm(high, table[1]) + mm(low, table[0]))


def table_left(table, value):
    high, low = halves(value)
    return mm(table[0], high) + (mm(table[1], high) + mm(table[0], low))


def split_rows(value):
    sums, differences = [], []
    for n in range(2):
        low = jnp.concatenate([value[256 * n + 64 * h :][:32] for h in range(4)], axis=0)
        high = jnp.concatenate([value[256 * n + 64 * h + 32 :][:32] for h in range(4)], axis=0)
        for out, part in ((sums, low + high), (differences, low - high)):
            out.append(jnp.concatenate([part[:, :128], part[:, 128:]], axis=0))
    return jnp.concatenate(sums, axis=1), jnp.concatenate(differences, axis=1)


def join_rows(even, odd):
    low, high = even + odd, even - odd
    pieces = []
    for n in range(2):
        first = slice(128 * n, 128 * n + 128)
        parts = [jnp.concatenate([p[:128, first], p[128:, first]], axis=1) for p in (low, high)]
        for h in range(4):
            for part in parts:
                pieces.append(part[32 * h : 32 * h + 32])
    return jnp.concatenate(pieces, axis=0)


def coded(value):
    peak = jnp.maximum(jnp.max(jnp.abs(value), axis=1, keepdims=True), 1e-30)
    code = jnp.round(value * (32767.0 / peak)).astype(jnp.int32).astype(jnp.int16)
    return code, peak[:, 0]


def decoded(code, peak):
    return code.astype(jnp.int32).astype(f32) * (peak * (1.0 / 32767.0))[:, None]


def folded(value):
    return value.reshape(-1, 8, 128).sum(axis=0)


def decode_all(i):
    return {
        "x": i // 64,
        "k": lax.rem(i // 32, 2),
        "y": lax.rem(i // 8, 4),
        "g": lax.rem(i // 2, 4),
        "b": lax.rem(i, 2),
    }


def lanes(shape):
    return lax.broadcasted_iota(jnp.int32, shape, len(shape) - 1)


def plane_shift(value, dz):
    if dz == 0:
        return value
    if dz < 0:
        edge = pltpu.roll(value[:, -128:], 64, 1)
        edge = jnp.where(lanes(edge.shape) >= 64, edge, 0.0)
        return jnp.concatenate([edge, value[:, :-128]], axis=1)
    edge = pltpu.roll(value[:, :128], 64, 1)
    edge = jnp.where(lanes(edge.shape) < 64, edge, 0.0)
    return jnp.concatenate([value[:, 128:], edge], axis=1)


def column_shift(value, dx):
    if dx == 0:
        return value
    width = value.shape[1]
    column = lax.rem(lanes(value.shape), 64)
    if dx < 0:
        return jnp.where(column != 0, pltpu.roll(value, 1, 1), 0.0)
    return jnp.where(column != 63, pltpu.roll(value, width - 1, 1), 0.0)


def step_kernel(
    prior_ref,
    k_hbm,
    m_hbm,
    mask_ref,
    w1_ref,
    w2_ref,
    w3_ref,
    b1_ref,
    b2_ref,
    b3_ref,
    fy_ref,
    gy_ref,
    fz_ref,
    gz_ref,
    out_ref,
    k_ref,
    m_ref,
    s_ref,
    feat,
    fbuf,
    f_rows,
    a1,
    h1m,
    h1e,
    p3,
    dplanes,
    dsrc,
    dbuf,
    osrc,
    obuf,
    acc,
    mask_all,
    mask_t,
    spectra,
    out_code,
    out_peak,
    part_code,
    part_peak,
    own_code,
    own_peak,
    full_code,
    full_peak,
    full,
    stat_a,
    stat_b,
    stat_c,
    stat_own,
    send_sem,
    part_sem,
    full_sem,
    mask_sem,
    stat_sem_a,
    stat_sem_b,
    stat_sem_c,
    feat_send,
    feat_sem,
    bulk_send,
    bulk_sem,
    local_sem,
):
    x, k, y, g, b = (lax.axis_index(name) for name in AXES)
    slab = x * 2 + k
    line = g * 2 + b
    me = x * 16 + k * 8 + y * 2 + b
    row = slab * 32 + y * 8 + line

    xs = [lax.rem(x + i, 4) for i in range(4)]
    ks = [k, 1 - k]
    ys = [lax.rem(y + i, 4) for i in range(4)]
    bs = [b, 1 - b]
    group = []
    for n in range(64):
        i, j = n % 4, n // 4 % 4
        offset = (i, (n // 16 + j) % 2, (i + j) % 4, (n // 32 + i) % 2)
        if any(offset):
            there = xs[offset[0]], ks[offset[1]], ys[offset[2]], bs[offset[3]]
            index = there[0] * 16 + there[1] * 8 + there[2] * 2 + there[3]
            group.append((index, dict(zip(GROUP, there))))

    def row_peer(i):
        return decode_all(lax.rem(row + 256 + i, 256))

    def slab_peer(i):
        t = lax.rem(slab + i, 8)
        return t, {"x": t // 2, "k": lax.rem(t, 2)}

    def y_peer(i):
        t = lax.rem(y + i, 4)
        return t, {"y": t}

    def line_peer(i):
        t = lax.rem(line + i, 8)
        return t, {"g": t // 2, "b": lax.rem(t, 2)}

    def g_peer(i):
        t = lax.rem(g + i, 4)
        return t, {"g": t}

    mesh_id = pl.DeviceIdType.MESH
    barrier = pltpu.get_barrier_semaphore()

    for _, device in group:
        pl.semaphore_signal(barrier, inc=1, device_id=device, device_id_type=mesh_id)
    for i in (-3, -2, -1, 1, 2, 3):
        pl.semaphore_signal(barrier, inc=1, device_id=row_peer(i), device_id_type=mesh_id)
    for i in range(1, 4):
        for c in range(2):
            pl.semaphore_signal(
                barrier,
                inc=1,
                device_id={"g": lax.rem(g + i, 4), "b": lax.rem(b + c, 2)},
                device_id_type=mesh_id,
            )
    feat[...] = prior_ref[...].astype(bf16)
    k_local = pltpu.make_async_copy(k_hbm.at[me], k_ref.at[me], local_sem.at[0])
    m_local = pltpu.make_async_copy(m_hbm.at[me], m_ref.at[me], local_sem.at[1])
    k_local.start()
    m_local.start()
    pl.semaphore_wait(barrier, 75)

    def copy_to(source, target, departure, arrival, device):
        copy = pltpu.make_async_remote_copy(
            src_ref=source,
            dst_ref=target,
            send_sem=departure,
            recv_sem=arrival,
            device_id=device,
            device_id_type=mesh_id,
        )
        copy.start()
        return copy

    def send(source, target, slot, arrival, device):
        return copy_to(source, target, send_sem.at[slot], arrival, device)

    def bulk(*jobs):
        for t, device in group:
            for which, source, target in jobs:
                copy_to(
                    source.at[t], target.at[me], bulk_send.at[which], bulk_sem.at[which], device
                )

    def bulk_wait(which, source, target):
        pltpu.make_async_copy(
            target.at[pl.ds(0, 63)], target.at[pl.ds(0, 63)], bulk_sem.at[which]
        ).wait()
        pltpu.make_async_copy(
            source.at[pl.ds(0, 63)], source.at[pl.ds(0, 63)], bulk_send.at[which]
        ).wait()

    feat_copies = []
    for n, i in enumerate((-1, 1, -2, 2, -3, 3)):
        feat_copies.append(
            copy_to(feat, fbuf.at[3 - i], feat_send.at[n], feat_sem.at[n], row_peer(i))
        )
    mask_copies = []
    for i in range(1, 8):
        mask_copies.append(
            send(mask_ref, mask_all.at[slab], i - 1, mask_sem.at[i - 1], slab_peer(i)[1])
        )
    mask_all[pl.ds(slab, 1)] = mask_ref[...][None]
    bulk((0, k_hbm, k_ref), (1, m_hbm, m_ref))

    fbuf[3] = feat[...]
    for copy in feat_copies:
        copy.wait()
    f_rows[14:16] = jnp.zeros((2, 8192), f32)
    for r in range(7):
        inside = jnp.logical_and(row + r >= 3, row + r < 259)
        f_rows[2 * r : 2 * r + 2] = jnp.where(inside, fbuf[r].astype(f32), 0.0)
    for dx in range(3):
        shifted = column_shift(f_rows[...], dx - 1)
        for dz in range(3):
            tap = dz * 3 + dx
            a1[16 * tap : 16 * tap + 16] = plane_shift(shifted, dz - 1).astype(bf16)

    bias_one = jnp.concatenate([b1_ref[...]] * 8, axis=1)
    bias_two = jnp.concatenate([b2_ref[...]] * 4, axis=1)
    lane = lanes((1, 256))
    hidden_row = row - 2 + jnp.minimum(lane // 32, 4)
    keep1 = jnp.where(jnp.logical_and(hidden_row >= 0, hidden_row < 256), 1.0, 0.0)
    lane = lanes((1, 128))
    hidden_row = row - 1 + jnp.minimum(lane // 32, 2)
    keep2 = jnp.where(jnp.logical_and(hidden_row >= 0, hidden_row < 256), 1.0, 0.0)
    h1e[...] = jnp.zeros_like(h1e)

    def layer_one(n, _):
        first = pl.multiple_of(n * 512, 512)
        block = lax.dot_general(
            a1[:, pl.ds(first, 512)],
            w1_ref[...],
            (((0,), (0,)), ((), ())),
            preferred_element_type=f32,
        )
        block = (jnp.maximum(block + bias_one, 0.0) * keep1).astype(bf16)
        h1m[pl.ds(pl.multiple_of(first + 128, 128), 512)] = block[:, :128]
        for dz in range(3):
            h1e[pl.ds(pl.multiple_of(first + 256 - 128 * dz, 128), 512), 32 * dz : 32 * dz + 32] = (
                block[:, 128 + 32 * dz : 160 + 32 * dz]
            )
        return 0

    lax.fori_loop(0, 16, layer_one, 0)
    zero = jnp.zeros((64, 128), bf16)
    h1m[0:64] = zero
    h1m[64:128] = h1m[128 + 8064 : 128 + 8128]
    h1m[128 + 8192 : 128 + 8256] = h1m[192:256]
    h1m[128 + 8256 : 128 + 8320] = zero
    h1e[128:192, 0:32] = jnp.zeros((64, 32), bf16)
    h1e[192:256, 0:32] = h1e[128 + 8064 : 128 + 8128, 32:64]
    return_rows = h1e[192:256, 32:64]
    h1e[128 + 8064 : 128 + 8128, 64:96] = return_rows
    h1e[128 + 8128 : 128 + 8192, 64:96] = jnp.zeros((64, 32), bf16)

    def layer_two(n, _):
        first = pl.multiple_of(n * 512, 512)
        low = jnp.concatenate(
            [
                h1m[pl.ds(first, 512)],
                h1m[pl.ds(pl.multiple_of(first + 128, 128), 512)],
                h1m[pl.ds(pl.multiple_of(first + 256, 128), 512)],
                h1e[pl.ds(pl.multiple_of(first + 128, 128), 512)],
            ],
            axis=1,
        )
        block = mm(low, w2_ref[...])
        column = lax.rem(lax.broadcasted_iota(jnp.int32, (512, 128), 0), 64)
        block = (
            jnp.where(column != 0, pltpu.roll(block[:, :128], 1, 0), 0.0)
            + block[:, 128:256]
            + jnp.where(column != 63, pltpu.roll(block[:, 256:], 511, 0), 0.0)
        )
        block = (jnp.maximum(block + bias_two, 0.0) * keep2).astype(bf16)
        p3[:, pl.ds(first, 512)] = lax.dot_general(
            w3_ref[...], block, (((1,), (1,)), ((), ())), preferred_element_type=f32
        )
        return 0

    lax.fori_loop(0, 16, layer_two, 0)
    total = jnp.zeros((8, 8192), f32)
    for dx in range(3):
        side = jnp.zeros((8, 8192), f32)
        for dz in range(3):
            tap = dz * 3 + dx
            side = side + plane_shift(p3[8 * tap : 8 * tap + 8], dz - 1)
        total = total + column_shift(side, dx - 1)
    channel = lax.broadcasted_iota(jnp.int32, (2, 1), 0)
    total = total[0:2] + (prior_ref[...] + jnp.where(channel == 0, b3_ref[0], b3_ref[1]))
    for i in range(64):
        for c in range(2):
            dplanes[c, i : i + 1] = total[c : c + 1, 128 * i : 128 * i + 128]
    for c in range(2):
        turned = jnp.transpose(dplanes[c])
        dsrc[:, c] = jnp.concatenate([turned[:64], turned[64:]], axis=1)
    bulk((2, dsrc, dbuf))
    dbuf[pl.ds(me, 1)] = dsrc[pl.ds(me, 1)]

    acc[...] = jnp.zeros_like(acc)

    def maps_of(j):
        return s_ref[j, 0], s_ref[j, 1]

    def add_image(image, pair):
        for n in range(2):
            real, imag = maps_of(2 * pair + n)
            a_real = image[256 * n : 256 * n + 256, :128]
            a_imag = image[256 * n : 256 * n + 256, 128:]
            acc[0] += real * a_real + imag * a_imag
            acc[1] += real * a_imag - imag * a_real

    k_local.wait()
    m_local.wait()
    bulk_wait(0, k_hbm, k_ref)
    bulk_wait(1, m_hbm, m_ref)

    for copy in mask_copies:
        copy.wait()
    half = lax.broadcasted_iota(jnp.int32, (256, 256), 0)
    eye = (half == lax.broadcasted_iota(jnp.int32, (256, 256), 1)).astype(bf16)
    mask_rows = mask_all[...].reshape(128, 256)
    by_line = (((1,), (1,)), ((), ()))
    mask_t[...] = lax.dot_general(eye, mask_rows, by_line, preferred_element_type=f32)

    def adjoint_pair(pair, _):
        sides = []
        for p in range(2):
            cells = slice(128 * p, 128 * p + 128)
            planes = []
            for n in range(2):
                for c in range(2):
                    plane = jnp.concatenate(
                        [k_ref[8 * s + 2 * pair + n, c][:, cells] for s in range(8)], axis=0
                    )
                    planes.append(plane * mask_rows[:, cells])
            spectrum = jnp.concatenate(
                [
                    jnp.concatenate(planes[0:2], axis=1),
                    jnp.concatenate(planes[2:4], axis=1),
                ],
                axis=0,
            )
            sides.append(
                lax.dot_general(gy_ref[p, 0], spectrum, by_line, preferred_element_type=f32)
                + lax.dot_general(gy_ref[p, 1], spectrum, by_line, preferred_element_type=f32)
            )
        for n in range(2):
            j = 2 * pair + n
            for c in range(2):
                for h in range(4):
                    for s in range(8):
                        first = h * 64 + s * 8
                        s_ref[j, c, first : first + 8] = m_ref[8 * s + j, c, h].astype(f32)
        add_image(table_right(join_rows(*sides), gz_ref), pair)
        return 0

    lax.fori_loop(0, 4, adjoint_pair, 0)

    mine = pl.ds(pl.multiple_of(g * 64, 64), 64)

    def reduce_scatter(step):
        copies = []
        for i in range(1, 4):
            t, device = g_peer(i)
            code, peak = coded(acc[:, pl.ds(pl.multiple_of(t * 64, 64), 64)])
            out_code[step, i - 1] = code
            out_peak[step, i - 1] = peak
            for n, (source, target) in enumerate(((out_code, part_code), (out_peak, part_peak))):
                copies.append(
                    send(
                        source.at[step, i - 1],
                        target.at[step, i - 1],
                        13 + 2 * i + n,
                        part_sem.at[step, i - 1, n],
                        device,
                    )
                )

        def finish():
            for copy in copies:
                copy.wait()
            total = acc[:, mine]
            for i in range(3):
                total = total + decoded(part_code[step, i], part_peak[step, i])
            return total

        return finish

    def gather(step, value):
        code, peak = coded(value)
        own_code[step] = code
        own_peak[step] = peak
        copies = []
        for i in range(1, 4):
            _, device = g_peer(i)
            for n, (source, target) in enumerate(((own_code, full_code), (own_peak, full_peak))):
                copies.append(
                    send(
                        source.at[step],
                        target.at[step, g],
                        13 + 2 * i + n,
                        full_sem.at[step, i - 1, n],
                        device,
                    )
                )
        full[:, mine] = value

        def finish():
            for copy in copies:
                copy.wait()
            for i in range(1, 4):
                t, _ = g_peer(i)
                full[:, pl.ds(pl.multiple_of(t * 64, 64), 64)] = decoded(
                    full_code[step, t], full_peak[step, t]
                )

        return finish

    def forward_pair(pair, energy):
        d_real, d_imag = full[0], full[1]
        pieces = []
        for n in range(2):
            real, imag = maps_of(2 * pair + n)
            pieces.append(
                jnp.concatenate(
                    [real * d_real - imag * d_imag, real * d_imag + imag * d_real], axis=1
                )
            )
        sides = split_rows(table_right(jnp.concatenate(pieces, axis=0), fz_ref))
        for p in range(2):
            mask = mask_t[128 * p : 128 * p + 128]
            mask = jnp.concatenate([mask, mask], axis=1)
            mask = jnp.concatenate([mask, mask], axis=0)
            spectrum = table_left(fy_ref[p], sides[p]) * mask
            squares = spectrum * spectrum
            energy = energy + folded(squares[:, :128] + squares[:, 128:])
            high, low = halves(spectrum)
            spectra[pair, p, 0] = high
            spectra[pair, p, 1] = low
        return energy

    def inverse_pair(pair, _):
        sides = []
        for p in range(2):
            high, low = spectra[pair, p, 0], spectra[pair, p, 1]
            sides.append(mm(gy_ref[p, 0], high) + (mm(gy_ref[p, 1], high) + mm(gy_ref[p, 0], low)))
        add_image(table_right(join_rows(*sides), gz_ref), pair)
        return 0

    stages = (
        (8, slab_peer, slab, stat_a, stat_sem_a),
        (4, y_peer, y, stat_b, stat_sem_b),
        (8, line_peer, line, stat_c, stat_sem_c),
    )

    def totals(step, stage, value):
        count, peer, here, slots, sems = stages[stage]
        stat_own[step, stage] = value
        slots[step, pl.ds(here, 1)] = value[None]
        copies = []
        for i in range(1, count):
            copies.append(
                send(
                    stat_own.at[step, stage],
                    slots.at[step, here],
                    7 + i,
                    sems.at[step, i - 1],
                    peer(i)[1],
                )
            )

        def finish():
            for copy in copies:
                copy.wait()
            value = slots[step, 0]
            for i in range(1, count):
                value = value + slots[step, i]
            return value

        return finish

    def norm_of(value):
        return folded((value * value).reshape(128, 128))

    def operator(step, direction):
        finish = gather(step, direction)
        norm = norm_of(direction)
        finish()
        energy = lax.fori_loop(0, 4, forward_pair, jnp.zeros((8, 128), f32))
        acc[...] = jnp.zeros_like(acc)
        finish = totals(step, 0, jnp.stack([norm, energy]))
        lax.fori_loop(0, 2, inverse_pair, 0)
        finish = totals(step, 1, finish())
        lax.fori_loop(2, 4, inverse_pair, 0)
        image = reduce_scatter(step + 1)
        finish = totals(step, 2, finish())
        value = finish()
        norm, energy = jnp.sum(value[0]), jnp.sum(value[1])
        return norm, energy + penalty * norm, image() + penalty * direction

    right = reduce_scatter(0)()
    bulk_wait(2, dsrc, dbuf)
    right = right + penalty * jnp.stack([dbuf[:, 0], dbuf[:, 1]])
    rr, curvature, image = operator(0, right)
    alpha = rr / curvature
    residual = right - alpha * image
    fresh, curvature, second = operator(1, residual)
    growth = fresh / rr
    step_size = fresh / (curvature - growth * fresh / alpha)
    q = second + growth * image
    answer = alpha * right + step_size * (residual + growth * right)
    rest = residual - step_size * q
    for c in range(2):
        osrc[:, c] = answer[c]
        osrc[:, 2 + c] = rest[c]
    bulk((3, osrc, obuf))
    obuf[pl.ds(me, 1)] = osrc[pl.ds(me, 1)]
    bulk_wait(3, osrc, obuf)
    out_ref[0] = jnp.transpose(jnp.concatenate([obuf[:, 0], obuf[:, 1]], axis=0))
    out_ref[1] = jnp.transpose(jnp.concatenate([obuf[:, 2], obuf[:, 3]], axis=0))


def body(
    prior_image,
    coil_maps,
    kspace,
    sampling,
    weight_first,
    bias_first,
    weight_middle,
    bias_middle,
    weight_last,
    bias_last,
):
    mask = sampling.astype(bf16).reshape(16, 128, 2).transpose(0, 2, 1).reshape(16, 256)
    spectrum = kspace[0].reshape(16, 128, 2, 2, 64).transpose(4, 3, 0, 2, 1).reshape(64, 2, 16, 256)
    maps = coil_maps[0].reshape(4, 4, 2, 128, 2, 64).transpose(5, 4, 1, 0, 2, 3)
    maps = maps.reshape(64, 2, 4, 8, 128)
    prior = prior_image.reshape(2, 64, 2, 64).transpose(2, 1, 0, 3).reshape(2, 8192)

    first = weight_first.transpose(1, 2, 0, 4, 3).reshape(9, 6, 32)
    pieces = [jnp.pad(first, ((0, 0), (2 * r, 10 - 2 * r), (0, 0))) for r in (0, 1, 2, 3, 4, 4, 4)]
    w1 = jnp.pad(jnp.concatenate(pieces, axis=2), ((0, 0), (0, 0), (0, 32))).reshape(144, 256)
    middle = weight_middle.transpose(1, 0, 4, 2, 3).reshape(3, 96, 3, 32)
    pieces = [jnp.pad(middle, ((0, 0), (32 * r, 64 - 32 * r), (0, 0), (0, 0))) for r in range(3)]
    middle = jnp.concatenate(pieces + [jnp.zeros_like(pieces[0])], axis=3).reshape(3, 160, 384)
    w2 = jnp.concatenate(
        [
            middle[:, :128].reshape(384, 384),
            middle[:, 128:].reshape(96, 384),
            jnp.zeros((32, 384), bf16),
        ],
        axis=0,
    )
    w3 = weight_last.transpose(1, 2, 3, 0, 4).reshape(9, 2, 96)
    w3 = jnp.pad(w3, ((0, 0), (0, 6), (0, 32))).reshape(72, 128)
    b1 = bias_first[None]
    b2 = bias_middle[None]

    forward, backward, z_forward, z_backward = tables()
    vmem = pl.BlockSpec(memory_space=pltpu.VMEM)
    hbm = pl.BlockSpec(memory_space=pl.ANY)
    out = jax.ShapeDtypeStruct((2, 128, 128), f32)
    smem = pl.BlockSpec(memory_space=pltpu.SMEM)
    dma = pltpu.SemaphoreType.DMA
    out = pl.pallas_call(
        step_kernel,
        out_shape=out,
        in_specs=[vmem] + [hbm] * 2 + [vmem] * 6 + [smem] + [vmem] * 4,
        out_specs=vmem,
        scratch_shapes=[
            pltpu.VMEM((64, 2, 16, 256), bf16),
            pltpu.VMEM((64, 2, 4, 8, 128), bf16),
            pltpu.VMEM((8, 2, 256, 128), f32),
            pltpu.VMEM((2, 8192), bf16),
            pltpu.VMEM((7, 2, 8192), bf16),
            pltpu.VMEM((16, 8192), f32),
            pltpu.VMEM((144, 8192), bf16),
            pltpu.VMEM((8448, 128), bf16),
            pltpu.VMEM((8448, 128), bf16),
            pltpu.VMEM((72, 8192), f32),
            pltpu.VMEM((2, 64, 128), f32),
            pltpu.VMEM((64, 2, 128), f32),
            pltpu.VMEM((64, 2, 128), f32),
            pltpu.VMEM((64, 4, 128), f32),
            pltpu.VMEM((64, 4, 128), f32),
            pltpu.VMEM((2, 256, 128), f32),
            pltpu.VMEM((8, 16, 256), bf16),
            pltpu.VMEM((256, 128), f32),
            pltpu.VMEM((4, 2, 2, 256, 256), bf16),
            pltpu.VMEM((3, 3, 2, 64, 128), jnp.int16),
            pltpu.VMEM((3, 3, 2, 128), f32),
            pltpu.VMEM((3, 3, 2, 64, 128), jnp.int16),
            pltpu.VMEM((3, 3, 2, 128), f32),
            pltpu.VMEM((2, 2, 64, 128), jnp.int16),
            pltpu.VMEM((2, 2, 128), f32),
            pltpu.VMEM((2, 4, 2, 64, 128), jnp.int16),
            pltpu.VMEM((2, 4, 2, 128), f32),
            pltpu.VMEM((2, 256, 128), f32),
            pltpu.VMEM((2, 8, 2, 8, 128), f32),
            pltpu.VMEM((2, 4, 2, 8, 128), f32),
            pltpu.VMEM((2, 8, 2, 8, 128), f32),
            pltpu.VMEM((2, 3, 2, 8, 128), f32),
            dma((22,)),
            dma((3, 3, 2)),
            dma((2, 3, 2)),
            dma((7,)),
            dma((2, 7)),
            dma((2, 3)),
            dma((2, 7)),
            dma((6,)),
            dma((6,)),
            dma((4,)),
            dma((4,)),
            dma((2,)),
        ],
        compiler_params=pltpu.CompilerParams(
            collective_id=0, has_side_effects=True, vmem_limit_bytes=60 * 1024 * 1024
        ),
    )(
        prior,
        spectrum,
        maps,
        mask,
        w1,
        w2,
        w3,
        b1,
        b2,
        bias_last,
        jnp.asarray(forward),
        jnp.asarray(backward),
        jnp.asarray(z_forward),
        jnp.asarray(z_backward),
    )
    return out[0:1], out[1:2]


def solution(mesh):
    torus = Mesh(mesh.devices.reshape(SIZES), AXES)
    coil = ("y", "g", "b")
    slab = ("x", "k")
    in_specs = (
        P(ALL, None, None),
        P(coil, slab, None, None),
        P(coil, slab, None, None),
        P(slab, None),
        P(),
        P(),
        P(),
        P(),
        P(),
        P(),
    )
    out_specs = (P(ALL, None, None), P(ALL, None, None))
    return jax.shard_map(body, mesh=torus, in_specs=in_specs, out_specs=out_specs, check_vma=False)
```

```python
import functools

import jax
import jax.numpy as jnp
import numpy as np
from jax import lax
from jax.experimental import pallas as pl
from jax.experimental.pallas import tpu as pltpu
from jax.sharding import Mesh
from jax.sharding import PartitionSpec as P

AXES = ("x", "k", "y", "g", "b")
SIZES = (4, 2, 4, 4, 2)
GROUP = ("x", "k", "y", "b")
ALL = ("x", "k", "y", "g", "b")

penalty = 0.5
f32 = jnp.float32
bf16 = jnp.bfloat16


def split_table(table):
    table = table.astype(np.float32)
    high = table.astype(jnp.bfloat16)
    low = (table - high.astype(np.float32)).astype(jnp.bfloat16)
    return np.stack([high, low])


def row_order():
    order = np.zeros(256, np.int64)
    for g in range(4):
        for s in range(8):
            for y in range(4):
                for b in range(2):
                    order[g * 64 + s * 8 + y * 2 + b] = s * 32 + y * 8 + 2 * g + b
    return order


def tables():
    rows = row_order().reshape(4, 2, 32)[:, 0].reshape(128)
    forward, backward = [], []
    for parity in range(2):
        angle = 2 * np.pi * (np.outer(2 * np.arange(128) + parity, rows) % 256) / 256
        c, s = np.cos(angle) / 16.0, np.sin(angle) / 16.0
        forward.append(split_table(np.block([[c, s], [-s, c]])))
        backward.append(split_table(np.block([[c.T, -s.T], [s.T, c.T]])))
    angle = 2 * np.pi * (np.outer(np.arange(128), np.arange(128)) % 128) / 128
    c, s = np.cos(angle) / np.sqrt(128.0), np.sin(angle) / np.sqrt(128.0)
    z_forward = split_table(np.block([[c, -s], [s, c]]))
    z_backward = split_table(np.block([[c, s], [-s, c]]))
    return np.stack(forward), np.stack(backward), z_forward, z_backward


def halves(value):
    high = value.astype(bf16)
    low = (value - high.astype(f32)).astype(bf16)
    return high, low


def mm(a, b):
    return jnp.dot(a, b, preferred_element_type=f32)


def three(left, right):
    return mm(left[0], right[0]) + (mm(left[0], right[1]) + mm(left[1], right[0]))


def coded(value):
    peak = jnp.maximum(jnp.max(jnp.abs(value), axis=1, keepdims=True), 1e-30)
    code = jnp.round(value * (32767.0 / peak)).astype(jnp.int32).astype(jnp.int16)
    return code, peak[:, 0]


def decoded(code, peak):
    return code.astype(jnp.int32).astype(f32) * (peak * (1.0 / 32767.0))[:, None]


def folded(value):
    return value.reshape(-1, 8, 128).sum(axis=0)


def decode_all(i):
    return {
        "x": i // 64,
        "k": lax.rem(i // 32, 2),
        "y": lax.rem(i // 8, 4),
        "g": lax.rem(i // 2, 4),
        "b": lax.rem(i, 2),
    }


def lanes(shape):
    return lax.broadcasted_iota(jnp.int32, shape, len(shape) - 1)


def plane_shift(value, dz):
    if dz == 0:
        return value
    if dz < 0:
        edge = pltpu.roll(value[:, -128:], 64, 1)
        edge = jnp.where(lanes(edge.shape) >= 64, edge, 0.0)
        return jnp.concatenate([edge, value[:, :-128]], axis=1)
    edge = pltpu.roll(value[:, :128], 64, 1)
    edge = jnp.where(lanes(edge.shape) < 64, edge, 0.0)
    return jnp.concatenate([value[:, 128:], edge], axis=1)


def column_shift(value, dx):
    if dx == 0:
        return value
    width = value.shape[1]
    column = lax.rem(lanes(value.shape), 64)
    if dx < 0:
        return jnp.where(column != 0, pltpu.roll(value, 1, 1), 0.0)
    return jnp.where(column != 63, pltpu.roll(value, width - 1, 1), 0.0)


def step_kernel(
    prior_ref,
    k_hbm,
    m_hbm,
    sampling_ref,
    w1_ref,
    w2_ref,
    w3_ref,
    b1_ref,
    b2_ref,
    b3_ref,
    fy_ref,
    gy_ref,
    fz_ref,
    gz_ref,
    out_ref,
    k_ref,
    m_ref,
    s_ref,
    cells,
    flat,
    feat,
    fbuf,
    f_rows,
    a1,
    h1m,
    h1e,
    p3,
    dplanes,
    dsrc,
    dbuf,
    osrc,
    obuf,
    mask_own,
    mask_all,
    mask_t,
    rows_in,
    spectra,
    rows_out,
    out_code,
    out_peak,
    part_code,
    part_peak,
    own_code,
    own_peak,
    full_code,
    full_peak,
    stat_a,
    stat_b,
    stat_c,
    stat_own,
    send_sem,
    part_sem,
    full_sem,
    mask_sem,
    stat_sem_a,
    stat_sem_b,
    stat_sem_c,
    feat_send,
    feat_sem,
    bulk_send,
    bulk_sem,
    local_sem,
):
    x, k, y, g, b = (lax.axis_index(name) for name in AXES)
    slab = x * 2 + k
    line = g * 2 + b
    me = x * 16 + k * 8 + y * 2 + b
    row = slab * 32 + y * 8 + line

    xs = [lax.rem(x + i, 4) for i in range(4)]
    ks = [k, 1 - k]
    ys = [lax.rem(y + i, 4) for i in range(4)]
    bs = [b, 1 - b]
    group = []
    for n in range(64):
        i, j = n % 4, n // 4 % 4
        offset = (i, (n // 16 + j) % 2, (i + j) % 4, (n // 32 + i) % 2)
        if any(offset):
            there = xs[offset[0]], ks[offset[1]], ys[offset[2]], bs[offset[3]]
            index = there[0] * 16 + there[1] * 8 + there[2] * 2 + there[3]
            group.append((index, dict(zip(GROUP, there))))

    def row_peer(i):
        return decode_all(lax.rem(row + 256 + i, 256))

    def slab_peer(i):
        t = lax.rem(slab + i, 8)
        return t, {"x": t // 2, "k": lax.rem(t, 2)}

    def y_peer(i):
        t = lax.rem(y + i, 4)
        return t, {"y": t}

    def line_peer(i):
        t = lax.rem(line + i, 8)
        return t, {"g": t // 2, "b": lax.rem(t, 2)}

    def g_peer(i):
        t = lax.rem(g + i, 4)
        return t, {"g": t}

    mesh_id = pl.DeviceIdType.MESH
    barrier = pltpu.get_barrier_semaphore()

    for _, device in group:
        pl.semaphore_signal(barrier, inc=1, device_id=device, device_id_type=mesh_id)
    for i in (-3, -2, -1, 1, 2, 3):
        pl.semaphore_signal(barrier, inc=1, device_id=row_peer(i), device_id_type=mesh_id)
    for i in range(1, 4):
        for c in range(2):
            pl.semaphore_signal(
                barrier,
                inc=1,
                device_id={"g": lax.rem(g + i, 4), "b": lax.rem(b + c, 2)},
                device_id_type=mesh_id,
            )
    mask_own[...] = sampling_ref[...].astype(f32).astype(bf16)
    left = lanes((64, 128)) < 64
    top, bottom = prior_ref[0:64], prior_ref[64:128]
    cells[0] = jnp.where(left, top, pltpu.roll(bottom, 64, 1))
    cells[1] = jnp.where(left, pltpu.roll(top, 64, 1), bottom)
    for i in range(64):
        for c in range(2):
            flat[c : c + 1, 128 * i : 128 * i + 128] = cells[c, i : i + 1]
    feat[...] = flat[...].astype(bf16)
    k_local = pltpu.make_async_copy(k_hbm.at[me], k_ref.at[me], local_sem.at[0])
    m_local = pltpu.make_async_copy(m_hbm.at[me], m_ref.at[me], local_sem.at[1])
    k_local.start()
    m_local.start()
    pl.semaphore_wait(barrier, 75)

    def copy_to(source, target, departure, arrival, device):
        copy = pltpu.make_async_remote_copy(
            src_ref=source,
            dst_ref=target,
            send_sem=departure,
            recv_sem=arrival,
            device_id=device,
            device_id_type=mesh_id,
        )
        copy.start()
        return copy

    def send(source, target, slot, arrival, device):
        return copy_to(source, target, send_sem.at[slot], arrival, device)

    def bulk(*jobs):
        for t, device in group:
            for which, source, target in jobs:
                copy_to(
                    source.at[t], target.at[me], bulk_send.at[which], bulk_sem.at[which], device
                )

    def bulk_wait(which, source, target):
        pltpu.make_async_copy(
            target.at[pl.ds(0, 63)], target.at[pl.ds(0, 63)], bulk_sem.at[which]
        ).wait()
        pltpu.make_async_copy(
            source.at[pl.ds(0, 63)], source.at[pl.ds(0, 63)], bulk_send.at[which]
        ).wait()

    feat_copies = []
    for n, i in enumerate((-1, 1, -2, 2, -3, 3)):
        feat_copies.append(
            copy_to(feat, fbuf.at[3 - i], feat_send.at[n], feat_sem.at[n], row_peer(i))
        )
    mask_copies = []
    for i in range(1, 8):
        mask_copies.append(
            send(mask_own, mask_all.at[slab], i - 1, mask_sem.at[i - 1], slab_peer(i)[1])
        )
    mask_all[pl.ds(slab, 1)] = mask_own[...][None]
    bulk((0, k_hbm, k_ref), (1, m_hbm, m_ref))

    fbuf[3] = feat[...]
    for copy in feat_copies:
        copy.wait()
    f_rows[14:16] = jnp.zeros((2, 8192), f32)
    for r in range(7):
        inside = jnp.logical_and(row + r >= 3, row + r < 259)
        f_rows[2 * r : 2 * r + 2] = jnp.where(inside, fbuf[r].astype(f32), 0.0)
    for dx in range(3):
        shifted = column_shift(f_rows[...], dx - 1)
        for dz in range(3):
            tap = dz * 3 + dx
            a1[16 * tap : 16 * tap + 16] = plane_shift(shifted, dz - 1).astype(bf16)

    bias_one = jnp.concatenate([b1_ref[...]] * 8, axis=1)
    bias_two = jnp.concatenate([b2_ref[...]] * 4, axis=1)
    lane = lanes((1, 256))
    hidden_row = row - 2 + jnp.minimum(lane // 32, 4)
    keep1 = jnp.where(jnp.logical_and(hidden_row >= 0, hidden_row < 256), 1.0, 0.0)
    lane = lanes((1, 128))
    hidden_row = row - 1 + jnp.minimum(lane // 32, 2)
    keep2 = jnp.where(jnp.logical_and(hidden_row >= 0, hidden_row < 256), 1.0, 0.0)
    h1e[...] = jnp.zeros_like(h1e)

    def layer_one(n, _):
        first = pl.multiple_of(n * 512, 512)
        block = lax.dot_general(
            a1[:, pl.ds(first, 512)],
            w1_ref[...],
            (((0,), (0,)), ((), ())),
            preferred_element_type=f32,
        )
        block = (jnp.maximum(block + bias_one, 0.0) * keep1).astype(bf16)
        h1m[pl.ds(pl.multiple_of(first + 128, 128), 512)] = block[:, :128]
        for dz in range(3):
            h1e[pl.ds(pl.multiple_of(first + 256 - 128 * dz, 128), 512), 32 * dz : 32 * dz + 32] = (
                block[:, 128 + 32 * dz : 160 + 32 * dz]
            )
        return 0

    lax.fori_loop(0, 16, layer_one, 0)
    zero = jnp.zeros((64, 128), bf16)
    h1m[0:64] = zero
    h1m[64:128] = h1m[128 + 8064 : 128 + 8128]
    h1m[128 + 8192 : 128 + 8256] = h1m[192:256]
    h1m[128 + 8256 : 128 + 8320] = zero
    h1e[128:192, 0:32] = jnp.zeros((64, 32), bf16)
    h1e[192:256, 0:32] = h1e[128 + 8064 : 128 + 8128, 32:64]
    return_rows = h1e[192:256, 32:64]
    h1e[128 + 8064 : 128 + 8128, 64:96] = return_rows
    h1e[128 + 8128 : 128 + 8192, 64:96] = jnp.zeros((64, 32), bf16)

    def layer_two(n, _):
        first = pl.multiple_of(n * 512, 512)
        low = jnp.concatenate(
            [
                h1m[pl.ds(first, 512)],
                h1m[pl.ds(pl.multiple_of(first + 128, 128), 512)],
                h1m[pl.ds(pl.multiple_of(first + 256, 128), 512)],
                h1e[pl.ds(pl.multiple_of(first + 128, 128), 512)],
            ],
            axis=1,
        )
        block = mm(low, w2_ref[...])
        column = lax.rem(lax.broadcasted_iota(jnp.int32, (512, 128), 0), 64)
        block = (
            jnp.where(column != 0, pltpu.roll(block[:, :128], 1, 0), 0.0)
            + block[:, 128:256]
            + jnp.where(column != 63, pltpu.roll(block[:, 256:], 511, 0), 0.0)
        )
        block = (jnp.maximum(block + bias_two, 0.0) * keep2).astype(bf16)
        p3[:, pl.ds(first, 512)] = lax.dot_general(
            w3_ref[...], block, (((1,), (1,)), ((), ())), preferred_element_type=f32
        )
        return 0

    lax.fori_loop(0, 16, layer_two, 0)
    total = jnp.zeros((8, 8192), f32)
    for dx in range(3):
        side = jnp.zeros((8, 8192), f32)
        for dz in range(3):
            tap = dz * 3 + dx
            side = side + plane_shift(p3[8 * tap : 8 * tap + 8], dz - 1)
        total = total + column_shift(side, dx - 1)
    for i in range(64):
        for c in range(2):
            dplanes[c, i : i + 1] = total[c : c + 1, 128 * i : 128 * i + 128]
    for c in range(2):
        turned = jnp.transpose(dplanes[c] + (cells[c] + b3_ref[c]))
        dsrc[:, c] = jnp.concatenate([turned[:64], turned[64:]], axis=1)
    bulk((2, dsrc, dbuf))
    dbuf[pl.ds(me, 1)] = dsrc[pl.ds(me, 1)]

    k_local.wait()
    m_local.wait()
    for copy in mask_copies:
        copy.wait()
    order = lax.broadcasted_iota(jnp.int32, (256, 256), 0)
    order = 2 * lax.rem(order, 128) + order // 128
    order = (order == lax.broadcasted_iota(jnp.int32, (256, 256), 1)).astype(bf16)
    mask_rows = mask_all[...].reshape(128, 256)
    by_line = (((1,), (1,)), ((), ()))
    mask_t[...] = lax.dot_general(order, mask_rows, by_line, preferred_element_type=f32)
    bulk_wait(0, k_hbm, k_ref)
    bulk_wait(1, m_hbm, m_ref)

    def put_rows(pair, even, odd):
        for h, part in ((0, even + odd), (1, even - odd)):
            for q, value in enumerate(halves(part)):
                for n in range(2):
                    first = slice(128 * n, 128 * n + 128)
                    piece = jnp.concatenate([value[:128, first], value[128:, first]], axis=1)
                    for i in range(4):
                        rows_out[q, i, 2 * pair + n, 32 * h : 32 * h + 32] = piece[
                            32 * i : 32 * i + 32
                        ]

    def adjoint_pair(pair, _):
        planes = []
        for n in range(2):
            for c in range(2):
                plane = jnp.concatenate(
                    [k_ref[8 * s + 2 * pair + n, c] for s in range(8)], axis=0
                )
                planes.append(plane * mask_rows)
        planes = lax.dot_general(
            jnp.concatenate(planes, axis=0), order, by_line, preferred_element_type=f32
        ).astype(bf16)
        sides = []
        for p in range(2):
            cell = slice(128 * p, 128 * p + 128)
            spectrum = jnp.concatenate(
                [
                    jnp.concatenate([planes[0:128, cell], planes[128:256, cell]], axis=1),
                    jnp.concatenate([planes[256:384, cell], planes[384:512, cell]], axis=1),
                ],
                axis=0,
            )
            sides.append(
                lax.dot_general(gy_ref[p, 0], spectrum, by_line, preferred_element_type=f32)
                + lax.dot_general(gy_ref[p, 1], spectrum, by_line, preferred_element_type=f32)
            )
        put_rows(pair, *sides)
        for n in range(2):
            j = 2 * pair + n
            for c in range(2):
                for h in range(4):
                    for s in range(8):
                        first = h * 64 + s * 8
                        s_ref[j, c, first : first + 8] = m_ref[8 * s + j, c, h].astype(f32)
        return 0

    lax.fori_loop(0, 4, adjoint_pair, 0, unroll=2)

    def maps_of(j, h):
        rows = pl.ds(pl.multiple_of(h * 64, 64), 64)
        return s_ref[j, 0, rows], s_ref[j, 1, rows]

    def image_rows(h):
        left = rows_out[0, h].reshape(512, 256), rows_out[1, h].reshape(512, 256)
        image = three(left, (gz_ref[0], gz_ref[1]))
        real_total, imag_total = 0.0, 0.0
        for j in range(8):
            real, imag = maps_of(j, h)
            a_real = image[64 * j : 64 * j + 64, :128]
            a_imag = image[64 * j : 64 * j + 64, 128:]
            real_total = real_total + (real * a_real + imag * a_imag)
            imag_total = imag_total + (real * a_imag - imag * a_real)
        return jnp.stack([real_total, imag_total])

    def reduce_scatter(step, between=lambda: None):
        copies = []
        for i in (2, 1, 3):
            t, device = g_peer(i)
            code, peak = coded(image_rows(t))
            out_code[step, i - 1] = code
            out_peak[step, i - 1] = peak
            for n, (source, target) in enumerate(((out_code, part_code), (out_peak, part_peak))):
                copies.append(
                    send(
                        source.at[step, i - 1],
                        target.at[step, i - 1],
                        13 + 2 * i + n,
                        part_sem.at[step, i - 1, n],
                        device,
                    )
                )
        between()
        total = image_rows(g)

        def finish():
            for copy in copies:
                copy.wait()
            value = total
            for i in range(3):
                value = value + decoded(part_code[step, i], part_peak[step, i])
            return value

        return finish

    def gather(step, value):
        code, peak = coded(value)
        own_code[step] = code
        own_peak[step] = peak
        copies = {}
        for i in (2, 1, 3):
            _, device = g_peer(i)
            copies[i] = [
                send(
                    source.at[step],
                    target.at[step, g],
                    13 + 2 * i + n,
                    full_sem.at[step, i - 1, n],
                    device,
                )
                for n, (source, target) in enumerate(((own_code, full_code), (own_peak, full_peak)))
            ]

        def finish(i):
            for copy in copies[i]:
                copy.wait()
            t = lax.rem(g + 4 - i, 4)
            return t, decoded(full_code[step, t], full_peak[step, t])

        return finish

    def forward_rows(h, value):
        pieces = []
        for j in range(8):
            real, imag = maps_of(j, h)
            pieces.append(
                jnp.concatenate(
                    [
                        real * value[0] - imag * value[1],
                        real * value[1] + imag * value[0],
                    ],
                    axis=1,
                )
            )
        lines = three(halves(jnp.concatenate(pieces, axis=0)), (fz_ref[0], fz_ref[1]))
        for j in range(8):
            low, high = lines[64 * j : 64 * j + 32], lines[64 * j + 32 : 64 * j + 64]
            place = slice(128 * (j % 2), 128 * (j % 2) + 128)
            for p, part in enumerate((low + high, low - high)):
                for q, piece in enumerate(halves(part)):
                    for c in range(2):
                        rows_in[q, j // 2, p, c, h, :, place] = piece[:, 128 * c : 128 * c + 128]

    def forward_pair(pair, energy):
        for p in range(2):
            mask = mask_t[128 * p : 128 * p + 128]
            mask = jnp.concatenate([mask, mask], axis=1)
            mask = jnp.concatenate([mask, mask], axis=0)
            sides = [rows_in[q, pair, p].reshape(256, 256) for q in range(2)]
            spectrum = three((fy_ref[p, 0], fy_ref[p, 1]), sides) * mask
            squares = spectrum * spectrum
            energy = energy + folded(squares[:, :128] + squares[:, 128:])
            high, low = halves(spectrum)
            spectra[pair, p, 0] = high
            spectra[pair, p, 1] = low
        return energy

    def inverse_pair(pair, _):
        sides = []
        for p in range(2):
            right = spectra[pair, p, 0], spectra[pair, p, 1]
            sides.append(three((gy_ref[p, 0], gy_ref[p, 1]), right))
        put_rows(pair, *sides)
        return 0

    stages = (
        (8, slab_peer, slab, stat_a, stat_sem_a),
        (4, y_peer, y, stat_b, stat_sem_b),
        (8, line_peer, line, stat_c, stat_sem_c),
    )

    def totals(step, stage, value):
        count, peer, here, slots, sems = stages[stage]
        stat_own[step, stage] = value
        slots[step, pl.ds(here, 1)] = value[None]
        copies = []
        for i in range(1, count):
            copies.append(
                send(
                    stat_own.at[step, stage],
                    slots.at[step, here],
                    7 + i,
                    sems.at[step, i - 1],
                    peer(i)[1],
                )
            )

        def finish():
            for copy in copies:
                copy.wait()
            value = slots[step, 0]
            for i in range(1, count):
                value = value + slots[step, i]
            return value

        return finish

    def norm_of(value):
        return folded((value * value).reshape(128, 128))

    def operator(step, direction):
        finish = gather(step, direction)
        norm = norm_of(direction)
        forward_rows(g, direction)
        for i in (1, 3, 2):
            forward_rows(*finish(i))
        energy = lax.fori_loop(0, 4, forward_pair, jnp.zeros((8, 128), f32), unroll=2)
        finish_a = totals(step, 0, jnp.stack([norm, energy]))
        lax.fori_loop(0, 4, inverse_pair, 0, unroll=2)
        finish_b = totals(step, 1, finish_a())
        last = []
        image = reduce_scatter(
            step + 1, lambda: last.append(totals(step, 2, finish_b()))
        )
        value = last[0]()
        norm, energy = jnp.sum(value[0]), jnp.sum(value[1])
        return norm, energy + penalty * norm, image() + penalty * direction

    right = reduce_scatter(0)()
    bulk_wait(2, dsrc, dbuf)
    right = right + penalty * jnp.stack([dbuf[:, 0], dbuf[:, 1]])
    rr, curvature, image = operator(0, right)
    alpha = rr / curvature
    residual = right - alpha * image
    fresh, curvature, second = operator(1, residual)
    growth = fresh / rr
    step_size = fresh / (curvature - growth * fresh / alpha)
    q = second + growth * image
    answer = alpha * right + step_size * (residual + growth * right)
    rest = residual - step_size * q
    for c in range(2):
        osrc[:, c] = answer[c]
        osrc[:, 2 + c] = rest[c]
    bulk((3, osrc, obuf))
    obuf[pl.ds(me, 1)] = osrc[pl.ds(me, 1)]
    bulk_wait(3, osrc, obuf)
    out_ref[0] = jnp.transpose(jnp.concatenate([obuf[:, 0], obuf[:, 1]], axis=0))
    out_ref[1] = jnp.transpose(jnp.concatenate([obuf[:, 2], obuf[:, 3]], axis=0))


def body(
    prior_image,
    coil_maps,
    kspace,
    sampling,
    weight_first,
    bias_first,
    weight_middle,
    bias_middle,
    weight_last,
    bias_last,
):
    spectrum = kspace[0].reshape(16, 256, 2, 64).transpose(3, 2, 0, 1)
    maps = coil_maps[0].reshape(4, 4, 2, 128, 2, 64).transpose(5, 4, 1, 0, 2, 3)
    maps = maps.reshape(64, 2, 4, 8, 128)

    first = weight_first.transpose(1, 2, 0, 4, 3).reshape(9, 6, 32)
    pieces = [jnp.pad(first, ((0, 0), (2 * r, 10 - 2 * r), (0, 0))) for r in (0, 1, 2, 3, 4, 4, 4)]
    w1 = jnp.pad(jnp.concatenate(pieces, axis=2), ((0, 0), (0, 0), (0, 32))).reshape(144, 256)
    middle = weight_middle.transpose(1, 0, 4, 2, 3).reshape(3, 96, 3, 32)
    pieces = [jnp.pad(middle, ((0, 0), (32 * r, 64 - 32 * r), (0, 0), (0, 0))) for r in range(3)]
    middle = jnp.concatenate(pieces + [jnp.zeros_like(pieces[0])], axis=3).reshape(3, 160, 384)
    w2 = jnp.concatenate(
        [
            middle[:, :128].reshape(384, 384),
            middle[:, 128:].reshape(96, 384),
            jnp.zeros((32, 384), bf16),
        ],
        axis=0,
    )
    w3 = weight_last.transpose(1, 2, 3, 0, 4).reshape(9, 2, 96)
    w3 = jnp.pad(w3, ((0, 0), (0, 6), (0, 32))).reshape(72, 128)
    b1 = bias_first[None]
    b2 = bias_middle[None]

    forward, backward, z_forward, z_backward = tables()
    vmem = pl.BlockSpec(memory_space=pltpu.VMEM)
    hbm = pl.BlockSpec(memory_space=pl.ANY)
    out = jax.ShapeDtypeStruct((2, 128, 128), f32)
    smem = pl.BlockSpec(memory_space=pltpu.SMEM)
    dma = pltpu.SemaphoreType.DMA
    out = pl.pallas_call(
        step_kernel,
        out_shape=out,
        in_specs=[vmem] + [hbm] * 2 + [vmem] * 6 + [smem] + [vmem] * 4,
        out_specs=vmem,
        scratch_shapes=[
            pltpu.VMEM((64, 2, 16, 256), bf16),
            pltpu.VMEM((64, 2, 4, 8, 128), bf16),
            pltpu.VMEM((8, 2, 256, 128), f32),
            pltpu.VMEM((2, 64, 128), f32),
            pltpu.VMEM((2, 8192), f32),
            pltpu.VMEM((2, 8192), bf16),
            pltpu.VMEM((7, 2, 8192), bf16),
            pltpu.VMEM((16, 8192), f32),
            pltpu.VMEM((144, 8192), bf16),
            pltpu.VMEM((8448, 128), bf16),
            pltpu.VMEM((8448, 128), bf16),
            pltpu.VMEM((72, 8192), f32),
            pltpu.VMEM((2, 64, 128), f32),
            pltpu.VMEM((64, 2, 128), f32),
            pltpu.VMEM((64, 2, 128), f32),
            pltpu.VMEM((64, 4, 128), f32),
            pltpu.VMEM((64, 4, 128), f32),
            pltpu.VMEM((16, 256), bf16),
            pltpu.VMEM((8, 16, 256), bf16),
            pltpu.VMEM((256, 128), f32),
            pltpu.VMEM((2, 4, 2, 2, 4, 32, 256), bf16),
            pltpu.VMEM((4, 2, 2, 256, 256), bf16),
            pltpu.VMEM((2, 4, 8, 64, 256), bf16),
            pltpu.VMEM((3, 3, 2, 64, 128), jnp.int16),
            pltpu.VMEM((3, 3, 2, 128), f32),
            pltpu.VMEM((3, 3, 2, 64, 128), jnp.int16),
            pltpu.VMEM((3, 3, 2, 128), f32),
            pltpu.VMEM((2, 2, 64, 128), jnp.int16),
            pltpu.VMEM((2, 2, 128), f32),
            pltpu.VMEM((2, 4, 2, 64, 128), jnp.int16),
            pltpu.VMEM((2, 4, 2, 128), f32),
            pltpu.VMEM((2, 8, 2, 8, 128), f32),
            pltpu.VMEM((2, 4, 2, 8, 128), f32),
            pltpu.VMEM((2, 8, 2, 8, 128), f32),
            pltpu.VMEM((2, 3, 2, 8, 128), f32),
            dma((22,)),
            dma((3, 3, 2)),
            dma((2, 3, 2)),
            dma((7,)),
            dma((2, 7)),
            dma((2, 3)),
            dma((2, 7)),
            dma((6,)),
            dma((6,)),
            dma((4,)),
            dma((4,)),
            dma((2,)),
        ],
        compiler_params=pltpu.CompilerParams(
            collective_id=0, has_side_effects=True, vmem_limit_bytes=60 * 1024 * 1024
        ),
    )(
        prior_image[0],
        spectrum,
        maps,
        sampling,
        w1,
        w2,
        w3,
        b1,
        b2,
        bias_last,
        jnp.asarray(forward),
        jnp.asarray(backward),
        jnp.asarray(z_forward),
        jnp.asarray(z_backward),
    )
    return out[0:1], out[1:2]


def solution(mesh):
    torus = Mesh(mesh.devices.reshape(SIZES), AXES)
    coil = ("y", "g", "b")
    slab = ("x", "k")
    in_specs = (
        P(ALL, None, None),
        P(coil, slab, None, None),
        P(coil, slab, None, None),
        P(slab, None),
        P(),
        P(),
        P(),
        P(),
        P(),
        P(),
    )
    out_specs = (P(ALL, None, None), P(ALL, None, None))
    return jax.shard_map(body, mesh=torus, in_specs=in_specs, out_specs=out_specs, check_vma=False)
```

```python
import functools

import jax
import jax.numpy as jnp
import numpy as np
from jax import lax
from jax.experimental import pallas as pl
from jax.experimental.pallas import tpu as pltpu
from jax.sharding import Mesh
from jax.sharding import PartitionSpec as P

AXES = ("x", "k", "y", "g", "b")
SIZES = (4, 2, 4, 4, 2)
GROUP = ("x", "k", "y", "b")
ALL = ("x", "k", "y", "g", "b")

penalty = 0.5
f32 = jnp.float32
bf16 = jnp.bfloat16


def split_table(table):
    table = table.astype(np.float32)
    high = table.astype(jnp.bfloat16)
    low = (table - high.astype(np.float32)).astype(jnp.bfloat16)
    return np.stack([high, low])


def row_order():
    order = np.zeros(256, np.int64)
    for g in range(4):
        for s in range(8):
            for y in range(4):
                for b in range(2):
                    order[g * 64 + s * 8 + y * 2 + b] = s * 32 + y * 8 + 2 * g + b
    return order


def tables():
    rows = row_order().reshape(4, 2, 32)[:, 0].reshape(128)
    forward, backward = [], []
    for parity in range(2):
        angle = 2 * np.pi * (np.outer(2 * np.arange(128) + parity, rows) % 256) / 256
        c, s = np.cos(angle) / 16.0, np.sin(angle) / 16.0
        forward.append(split_table(np.block([[c, s], [-s, c]])))
        backward.append(split_table(np.block([[c.T, -s.T], [s.T, c.T]])))
    angle = 2 * np.pi * (np.outer(np.arange(128), np.arange(128)) % 128) / 128
    c, s = np.cos(angle) / np.sqrt(128.0), np.sin(angle) / np.sqrt(128.0)
    z_forward = split_table(np.block([[c, -s], [s, c]]))
    z_backward = split_table(np.block([[c, s], [-s, c]]))
    return np.stack(forward), np.stack(backward), z_forward, z_backward


def halves(value):
    high = value.astype(bf16)
    low = (value - high.astype(f32)).astype(bf16)
    return high, low


def mm(a, b):
    return jnp.dot(a, b, preferred_element_type=f32)


def three(left, right):
    return mm(left[0], right[0]) + (mm(left[0], right[1]) + mm(left[1], right[0]))


def coded(value):
    peak = jnp.maximum(jnp.max(jnp.abs(value), axis=1, keepdims=True), 1e-30)
    code = jnp.round(value * (32767.0 / peak)).astype(jnp.int32).astype(jnp.int16)
    return code, peak[:, 0]


def decoded(code, peak):
    return code.astype(jnp.int32).astype(f32) * (peak * (1.0 / 32767.0))[:, None]


def folded(value):
    return value.reshape(-1, 8, 128).sum(axis=0)


def decode_all(i):
    return {
        "x": i // 64,
        "k": lax.rem(i // 32, 2),
        "y": lax.rem(i // 8, 4),
        "g": lax.rem(i // 2, 4),
        "b": lax.rem(i, 2),
    }


def lanes(shape):
    return lax.broadcasted_iota(jnp.int32, shape, len(shape) - 1)


def plane_shift(value, dz):
    if dz == 0:
        return value
    if dz < 0:
        edge = pltpu.roll(value[:, -128:], 64, 1)
        edge = jnp.where(lanes(edge.shape) >= 64, edge, 0.0)
        return jnp.concatenate([edge, value[:, :-128]], axis=1)
    edge = pltpu.roll(value[:, :128], 64, 1)
    edge = jnp.where(lanes(edge.shape) < 64, edge, 0.0)
    return jnp.concatenate([value[:, 128:], edge], axis=1)


def column_shift(value, dx):
    if dx == 0:
        return value
    width = value.shape[1]
    column = lax.rem(lanes(value.shape), 64)
    if dx < 0:
        return jnp.where(column != 0, pltpu.roll(value, 1, 1), 0.0)
    return jnp.where(column != 63, pltpu.roll(value, width - 1, 1), 0.0)


def step_kernel(
    prior_ref,
    k_hbm,
    m_hbm,
    sampling_ref,
    w1_ref,
    w2_ref,
    w3_ref,
    b1_ref,
    b2_ref,
    b3_ref,
    fy_ref,
    gy_ref,
    fz_ref,
    gz_ref,
    out_ref,
    k_ref,
    m_ref,
    s_ref,
    cells,
    flat,
    feat,
    fbuf,
    f_rows,
    a1,
    h1m,
    h1e,
    p3,
    dplanes,
    dsrc,
    dbuf,
    osrc,
    obuf,
    mask_own,
    mask_all,
    mask_t,
    rows_in,
    spectra,
    rows_out,
    out_code,
    out_peak,
    part_code,
    part_peak,
    own_code,
    own_peak,
    full_code,
    full_peak,
    stat_a,
    stat_c,
    stat_own,
    send_sem,
    part_sem,
    full_sem,
    mask_sem,
    stat_send,
    stat_sem_a,
    stat_sem_c,
    feat_send,
    feat_sem,
    bulk_send,
    bulk_sem,
    local_sem,
):
    x, k, y, g, b = (lax.axis_index(name) for name in AXES)
    slab = x * 2 + k
    line = g * 2 + b
    me = x * 16 + k * 8 + y * 2 + b
    row = slab * 32 + y * 8 + line

    xs = [lax.rem(x + i, 4) for i in range(4)]
    ks = [k, 1 - k]
    ys = [lax.rem(y + i, 4) for i in range(4)]
    bs = [b, 1 - b]
    group = []
    for n in range(64):
        i, j = n % 4, n // 4 % 4
        offset = (i, (n // 16 + j) % 2, (i + j) % 4, (n // 32 + i) % 2)
        if any(offset):
            there = xs[offset[0]], ks[offset[1]], ys[offset[2]], bs[offset[3]]
            index = there[0] * 16 + there[1] * 8 + there[2] * 2 + there[3]
            group.append((index, dict(zip(GROUP, there))))

    def row_peer(i):
        return decode_all(lax.rem(row + 256 + i, 256))

    def slab_peer(i):
        t = lax.rem(slab + i, 8)
        return t, {"x": t // 2, "k": lax.rem(t, 2)}

    def line_peer(i):
        t = lax.rem(line + i, 8)
        return t, {"g": t // 2, "b": lax.rem(t, 2)}

    def g_peer(i):
        t = lax.rem(g + i, 4)
        return t, {"g": t}

    mesh_id = pl.DeviceIdType.MESH
    barrier = pltpu.get_barrier_semaphore()

    for _, device in group:
        pl.semaphore_signal(barrier, inc=1, device_id=device, device_id_type=mesh_id)
    for i in (-3, -2, -1, 1, 2, 3):
        pl.semaphore_signal(barrier, inc=1, device_id=row_peer(i), device_id_type=mesh_id)
    for i in range(1, 4):
        for c in range(2):
            pl.semaphore_signal(
                barrier,
                inc=1,
                device_id={"g": lax.rem(g + i, 4), "b": lax.rem(b + c, 2)},
                device_id_type=mesh_id,
            )
    mask_own[...] = sampling_ref[...].astype(f32).astype(bf16)
    left = lanes((64, 128)) < 64
    top, bottom = prior_ref[0:64], prior_ref[64:128]
    cells[0] = jnp.where(left, top, pltpu.roll(bottom, 64, 1))
    cells[1] = jnp.where(left, pltpu.roll(top, 64, 1), bottom)
    for i in range(64):
        for c in range(2):
            flat[c : c + 1, 128 * i : 128 * i + 128] = cells[c, i : i + 1]
    feat[...] = flat[...].astype(bf16)
    k_local = pltpu.make_async_copy(k_hbm.at[me], k_ref.at[me], local_sem.at[0])
    m_local = pltpu.make_async_copy(m_hbm.at[me], m_ref.at[me], local_sem.at[1])
    k_local.start()
    m_local.start()
    pl.semaphore_wait(barrier, 75)

    def copy_to(source, target, departure, arrival, device):
        copy = pltpu.make_async_remote_copy(
            src_ref=source,
            dst_ref=target,
            send_sem=departure,
            recv_sem=arrival,
            device_id=device,
            device_id_type=mesh_id,
        )
        copy.start()
        return copy

    def send(source, target, slot, arrival, device):
        return copy_to(source, target, send_sem.at[slot], arrival, device)

    def bulk(*jobs):
        for t, device in group:
            for which, source, target in jobs:
                copy_to(
                    source.at[t], target.at[me], bulk_send.at[which], bulk_sem.at[which], device
                )

    def bulk_wait(which, source, target):
        pltpu.make_async_copy(
            target.at[pl.ds(0, 63)], target.at[pl.ds(0, 63)], bulk_sem.at[which]
        ).wait()
        pltpu.make_async_copy(
            source.at[pl.ds(0, 63)], source.at[pl.ds(0, 63)], bulk_send.at[which]
        ).wait()

    feat_copies = []
    for n, i in enumerate((-1, 1, -2, 2, -3, 3)):
        feat_copies.append(
            copy_to(feat, fbuf.at[3 - i], feat_send.at[n], feat_sem.at[n], row_peer(i))
        )
    mask_copies = []
    for i in range(1, 8):
        mask_copies.append(
            send(mask_own, mask_all.at[slab], i - 1, mask_sem.at[i - 1], slab_peer(i)[1])
        )
    mask_all[pl.ds(slab, 1)] = mask_own[...][None]
    bulk((0, k_hbm, k_ref))
    bulk((1, m_hbm, m_ref))

    fbuf[3] = feat[...]
    for copy in feat_copies:
        copy.wait()
    f_rows[14:16] = jnp.zeros((2, 8192), f32)
    for r in range(7):
        inside = jnp.logical_and(row + r >= 3, row + r < 259)
        f_rows[2 * r : 2 * r + 2] = jnp.where(inside, fbuf[r].astype(f32), 0.0)
    for dx in range(3):
        shifted = column_shift(f_rows[...], dx - 1)
        for dz in range(3):
            tap = dz * 3 + dx
            a1[16 * tap : 16 * tap + 16] = plane_shift(shifted, dz - 1).astype(bf16)

    bias_one = jnp.concatenate([b1_ref[...]] * 8, axis=1)
    bias_two = jnp.concatenate([b2_ref[...]] * 4, axis=1)
    lane = lanes((1, 256))
    hidden_row = row - 2 + jnp.minimum(lane // 32, 4)
    keep1 = jnp.where(jnp.logical_and(hidden_row >= 0, hidden_row < 256), 1.0, 0.0)
    lane = lanes((1, 128))
    hidden_row = row - 1 + jnp.minimum(lane // 32, 2)
    keep2 = jnp.where(jnp.logical_and(hidden_row >= 0, hidden_row < 256), 1.0, 0.0)
    h1e[...] = jnp.zeros_like(h1e)

    def layer_one(n, _):
        first = pl.multiple_of(n * 512, 512)
        block = lax.dot_general(
            a1[:, pl.ds(first, 512)],
            w1_ref[...],
            (((0,), (0,)), ((), ())),
            preferred_element_type=f32,
        )
        block = (jnp.maximum(block + bias_one, 0.0) * keep1).astype(bf16)
        h1m[pl.ds(pl.multiple_of(first + 128, 128), 512)] = block[:, :128]
        for dz in range(3):
            h1e[pl.ds(pl.multiple_of(first + 256 - 128 * dz, 128), 512), 32 * dz : 32 * dz + 32] = (
                block[:, 128 + 32 * dz : 160 + 32 * dz]
            )
        return 0

    lax.fori_loop(0, 16, layer_one, 0)
    zero = jnp.zeros((64, 128), bf16)
    h1m[0:64] = zero
    h1m[64:128] = h1m[128 + 8064 : 128 + 8128]
    h1m[128 + 8192 : 128 + 8256] = h1m[192:256]
    h1m[128 + 8256 : 128 + 8320] = zero
    h1e[128:192, 0:32] = jnp.zeros((64, 32), bf16)
    h1e[192:256, 0:32] = h1e[128 + 8064 : 128 + 8128, 32:64]
    return_rows = h1e[192:256, 32:64]
    h1e[128 + 8064 : 128 + 8128, 64:96] = return_rows
    h1e[128 + 8128 : 128 + 8192, 64:96] = jnp.zeros((64, 32), bf16)

    def layer_two(n, _):
        first = pl.multiple_of(n * 512, 512)
        low = jnp.concatenate(
            [
                h1m[pl.ds(first, 512)],
                h1m[pl.ds(pl.multiple_of(first + 128, 128), 512)],
                h1m[pl.ds(pl.multiple_of(first + 256, 128), 512)],
                h1e[pl.ds(pl.multiple_of(first + 128, 128), 512)],
            ],
            axis=1,
        )
        block = mm(low, w2_ref[...])
        column = lax.rem(lax.broadcasted_iota(jnp.int32, (512, 128), 0), 64)
        block = (
            jnp.where(column != 0, pltpu.roll(block[:, :128], 1, 0), 0.0)
            + block[:, 128:256]
            + jnp.where(column != 63, pltpu.roll(block[:, 256:], 511, 0), 0.0)
        )
        block = (jnp.maximum(block + bias_two, 0.0) * keep2).astype(bf16)
        p3[:, pl.ds(first, 512)] = lax.dot_general(
            w3_ref[...], block, (((1,), (1,)), ((), ())), preferred_element_type=f32
        )
        return 0

    lax.fori_loop(0, 16, layer_two, 0)
    total = jnp.zeros((8, 8192), f32)
    for dx in range(3):
        side = jnp.zeros((8, 8192), f32)
        for dz in range(3):
            tap = dz * 3 + dx
            side = side + plane_shift(p3[8 * tap : 8 * tap + 8], dz - 1)
        total = total + column_shift(side, dx - 1)
    for i in range(64):
        for c in range(2):
            dplanes[c, i : i + 1] = total[c : c + 1, 128 * i : 128 * i + 128]
    for c in range(2):
        turned = jnp.transpose(dplanes[c] + (cells[c] + b3_ref[c]))
        dsrc[:, c] = jnp.concatenate([turned[:64], turned[64:]], axis=1)
    bulk((2, dsrc, dbuf))
    dbuf[pl.ds(me, 1)] = dsrc[pl.ds(me, 1)]

    k_local.wait()
    for copy in mask_copies:
        copy.wait()
    order = lax.broadcasted_iota(jnp.int32, (256, 256), 0)
    order = 2 * lax.rem(order, 128) + order // 128
    order = (order == lax.broadcasted_iota(jnp.int32, (256, 256), 1)).astype(bf16)
    mask_rows = mask_all[...].reshape(128, 256)
    by_line = (((1,), (1,)), ((), ()))
    mask_t[...] = lax.dot_general(order, mask_rows, by_line, preferred_element_type=f32)
    bulk_wait(0, k_hbm, k_ref)

    def put_rows(pair, even, odd):
        for h, part in ((0, even + odd), (1, even - odd)):
            for q, value in enumerate(halves(part)):
                for n in range(2):
                    first = slice(128 * n, 128 * n + 128)
                    piece = jnp.concatenate([value[:128, first], value[128:, first]], axis=1)
                    for i in range(4):
                        rows_out[q, i, 2 * pair + n, 32 * h : 32 * h + 32] = piece[
                            32 * i : 32 * i + 32
                        ]

    def adjoint_pair(pair, _):
        planes = []
        for n in range(2):
            for c in range(2):
                plane = jnp.concatenate(
                    [k_ref[8 * s + 2 * pair + n, c] for s in range(8)], axis=0
                )
                planes.append(plane * mask_rows)
        planes = lax.dot_general(
            jnp.concatenate(planes, axis=0), order, by_line, preferred_element_type=f32
        ).astype(bf16)
        sides = []
        for p in range(2):
            cell = slice(128 * p, 128 * p + 128)
            spectrum = jnp.concatenate(
                [
                    jnp.concatenate([planes[0:128, cell], planes[128:256, cell]], axis=1),
                    jnp.concatenate([planes[256:384, cell], planes[384:512, cell]], axis=1),
                ],
                axis=0,
            )
            sides.append(
                lax.dot_general(gy_ref[p, 0], spectrum, by_line, preferred_element_type=f32)
                + lax.dot_general(gy_ref[p, 1], spectrum, by_line, preferred_element_type=f32)
            )
        put_rows(pair, *sides)
        return 0

    lax.fori_loop(0, 4, adjoint_pair, 0, unroll=2)
    m_local.wait()
    bulk_wait(1, m_hbm, m_ref)

    def widen_maps(j, _):
        for c in range(2):
            for h in range(4):
                for s in range(8):
                    first = h * 64 + s * 8
                    s_ref[j, c, first : first + 8] = m_ref[8 * s + j, c, h].astype(f32)
        return 0

    lax.fori_loop(0, 8, widen_maps, 0, unroll=2)

    def maps_of(j, h):
        rows = pl.ds(pl.multiple_of(h * 64, 64), 64)
        return s_ref[j, 0, rows], s_ref[j, 1, rows]

    def image_rows(h):
        left = rows_out[0, h].reshape(512, 256), rows_out[1, h].reshape(512, 256)
        image = three(left, (gz_ref[0], gz_ref[1]))
        real_total, imag_total = 0.0, 0.0
        for j in range(8):
            real, imag = maps_of(j, h)
            a_real = image[64 * j : 64 * j + 64, :128]
            a_imag = image[64 * j : 64 * j + 64, 128:]
            real_total = real_total + (real * a_real + imag * a_imag)
            imag_total = imag_total + (real * a_imag - imag * a_real)
        return jnp.stack([real_total, imag_total])

    def reduce_scatter(step, between=lambda: None):
        copies = []
        for i in (2, 1, 3):
            t, device = g_peer(i)
            code, peak = coded(image_rows(t))
            out_code[step, i - 1] = code
            out_peak[step, i - 1] = peak
            for n, (source, target) in enumerate(((out_code, part_code), (out_peak, part_peak))):
                copies.append(
                    send(
                        source.at[step, i - 1],
                        target.at[step, i - 1],
                        13 + 2 * i + n,
                        part_sem.at[step, i - 1, n],
                        device,
                    )
                )
        between()
        total = image_rows(g)

        def finish():
            for copy in copies:
                copy.wait()
            value = total
            for i in range(3):
                value = value + decoded(part_code[step, i], part_peak[step, i])
            return value

        return finish

    def gather(step, value):
        code, peak = coded(value)
        own_code[step] = code
        own_peak[step] = peak
        copies = {}
        for i in (2, 1, 3):
            _, device = g_peer(i)
            copies[i] = [
                send(
                    source.at[step],
                    target.at[step, g],
                    13 + 2 * i + n,
                    full_sem.at[step, i - 1, n],
                    device,
                )
                for n, (source, target) in enumerate(((own_code, full_code), (own_peak, full_peak)))
            ]

        def finish(i):
            for copy in copies[i]:
                copy.wait()
            t = lax.rem(g + 4 - i, 4)
            return t, decoded(full_code[step, t], full_peak[step, t])

        return finish

    def forward_rows(h, value):
        pieces = []
        for j in range(8):
            real, imag = maps_of(j, h)
            pieces.append(
                jnp.concatenate(
                    [
                        real * value[0] - imag * value[1],
                        real * value[1] + imag * value[0],
                    ],
                    axis=1,
                )
            )
        lines = three(halves(jnp.concatenate(pieces, axis=0)), (fz_ref[0], fz_ref[1]))
        for j in range(8):
            low, high = lines[64 * j : 64 * j + 32], lines[64 * j + 32 : 64 * j + 64]
            place = slice(128 * (j % 2), 128 * (j % 2) + 128)
            for p, part in enumerate((low + high, low - high)):
                for q, piece in enumerate(halves(part)):
                    for c in range(2):
                        rows_in[q, j // 2, p, c, h, :, place] = piece[:, 128 * c : 128 * c + 128]

    def forward_pair(pair, energy):
        for p in range(2):
            mask = mask_t[128 * p : 128 * p + 128]
            mask = jnp.concatenate([mask, mask], axis=1)
            mask = jnp.concatenate([mask, mask], axis=0)
            sides = [rows_in[q, pair, p].reshape(256, 256) for q in range(2)]
            spectrum = three((fy_ref[p, 0], fy_ref[p, 1]), sides) * mask
            squares = spectrum * spectrum
            energy = energy + folded(squares[:, :128] + squares[:, 128:])
            high, low = halves(spectrum)
            spectra[pair, p, 0] = high
            spectra[pair, p, 1] = low
        return energy

    def inverse_pair(pair, _):
        sides = []
        for p in range(2):
            right = spectra[pair, p, 0], spectra[pair, p, 1]
            sides.append(three((gy_ref[p, 0], gy_ref[p, 1]), right))
        put_rows(pair, *sides)
        return 0

    here = x * 8 + k * 4 + y
    plane = [
        {"x": xs[i], "k": ks[j], "y": ys[n]}
        for n in range(4)
        for j in range(2)
        for i in range(4)
        if i or j or n
    ]

    def plane_total(step, value):
        stat_own[step, 0] = value
        stat_a[step, pl.ds(here, 1)] = value[None]
        for device in plane:
            copy_to(
                stat_own.at[step, 0],
                stat_a.at[step, here],
                stat_send.at[step],
                stat_sem_a.at[step],
                device,
            )

        def finish():
            block = stat_a.at[step, pl.ds(0, 31)]
            pltpu.make_async_copy(block, block, stat_sem_a.at[step]).wait()
            pltpu.make_async_copy(block, block, stat_send.at[step]).wait()
            value = stat_a[step, 0]
            for i in range(1, 32):
                value = value + stat_a[step, i]
            return value

        return finish

    def line_total(step, value):
        stat_own[step, 1] = value
        stat_c[step, pl.ds(line, 1)] = value[None]
        copies = []
        for i in range(1, 8):
            copies.append(
                send(
                    stat_own.at[step, 1],
                    stat_c.at[step, line],
                    7 + i,
                    stat_sem_c.at[step, i - 1],
                    line_peer(i)[1],
                )
            )

        def finish():
            for copy in copies:
                copy.wait()
            value = stat_c[step, 0]
            for i in range(1, 8):
                value = value + stat_c[step, i]
            return value

        return finish

    def norm_of(value):
        return folded((value * value).reshape(128, 128))

    def operator(step, direction):
        finish = gather(step, direction)
        norm = norm_of(direction)
        forward_rows(g, direction)
        for i in (1, 3, 2):
            forward_rows(*finish(i))
        energy = lax.fori_loop(0, 4, forward_pair, jnp.zeros((8, 128), f32), unroll=2)
        stats = [jnp.sum(value, axis=0, keepdims=True) for value in (norm, energy)]
        finish_plane = plane_total(step, jnp.concatenate(stats, axis=0))
        lax.fori_loop(0, 4, inverse_pair, 0, unroll=2)
        last = []
        image = reduce_scatter(
            step + 1, lambda: last.append(line_total(step, finish_plane()))
        )
        value = last[0]()
        norm, energy = jnp.sum(value[0:1]), jnp.sum(value[1:2])
        return norm, energy + penalty * norm, image() + penalty * direction

    right = reduce_scatter(0)()
    bulk_wait(2, dsrc, dbuf)
    right = right + penalty * jnp.stack([dbuf[:, 0], dbuf[:, 1]])
    rr, curvature, image = operator(0, right)
    alpha = rr / curvature
    residual = right - alpha * image
    fresh, curvature, second = operator(1, residual)
    growth = fresh / rr
    step_size = fresh / (curvature - growth * fresh / alpha)
    q = second + growth * image
    answer = alpha * right + step_size * (residual + growth * right)
    rest = residual - step_size * q
    for c in range(2):
        osrc[:, c] = answer[c]
        osrc[:, 2 + c] = rest[c]
    bulk((3, osrc, obuf))
    obuf[pl.ds(me, 1)] = osrc[pl.ds(me, 1)]
    bulk_wait(3, osrc, obuf)
    out_ref[0] = jnp.transpose(jnp.concatenate([obuf[:, 0], obuf[:, 1]], axis=0))
    out_ref[1] = jnp.transpose(jnp.concatenate([obuf[:, 2], obuf[:, 3]], axis=0))


def body(
    prior_image,
    coil_maps,
    kspace,
    sampling,
    weight_first,
    bias_first,
    weight_middle,
    bias_middle,
    weight_last,
    bias_last,
):
    spectrum = kspace[0].reshape(16, 256, 2, 64).transpose(3, 2, 0, 1)
    maps = coil_maps[0].reshape(4, 4, 2, 128, 2, 64).transpose(5, 4, 1, 0, 2, 3)
    maps = maps.reshape(64, 2, 4, 8, 128)

    first = weight_first.transpose(1, 2, 0, 4, 3).reshape(9, 6, 32)
    pieces = [jnp.pad(first, ((0, 0), (2 * r, 10 - 2 * r), (0, 0))) for r in (0, 1, 2, 3, 4, 4, 4)]
    w1 = jnp.pad(jnp.concatenate(pieces, axis=2), ((0, 0), (0, 0), (0, 32))).reshape(144, 256)
    middle = weight_middle.transpose(1, 0, 4, 2, 3).reshape(3, 96, 3, 32)
    pieces = [jnp.pad(middle, ((0, 0), (32 * r, 64 - 32 * r), (0, 0), (0, 0))) for r in range(3)]
    middle = jnp.concatenate(pieces + [jnp.zeros_like(pieces[0])], axis=3).reshape(3, 160, 384)
    w2 = jnp.concatenate(
        [
            middle[:, :128].reshape(384, 384),
            middle[:, 128:].reshape(96, 384),
            jnp.zeros((32, 384), bf16),
        ],
        axis=0,
    )
    w3 = weight_last.transpose(1, 2, 3, 0, 4).reshape(9, 2, 96)
    w3 = jnp.pad(w3, ((0, 0), (0, 6), (0, 32))).reshape(72, 128)
    b1 = bias_first[None]
    b2 = bias_middle[None]

    forward, backward, z_forward, z_backward = tables()
    vmem = pl.BlockSpec(memory_space=pltpu.VMEM)
    hbm = pl.BlockSpec(memory_space=pl.ANY)
    out = jax.ShapeDtypeStruct((2, 128, 128), f32)
    smem = pl.BlockSpec(memory_space=pltpu.SMEM)
    dma = pltpu.SemaphoreType.DMA
    out = pl.pallas_call(
        step_kernel,
        out_shape=out,
        in_specs=[vmem] + [hbm] * 2 + [vmem] * 6 + [smem] + [vmem] * 4,
        out_specs=vmem,
        scratch_shapes=[
            pltpu.VMEM((64, 2, 16, 256), bf16),
            pltpu.VMEM((64, 2, 4, 8, 128), bf16),
            pltpu.VMEM((8, 2, 256, 128), f32),
            pltpu.VMEM((2, 64, 128), f32),
            pltpu.VMEM((2, 8192), f32),
            pltpu.VMEM((2, 8192), bf16),
            pltpu.VMEM((7, 2, 8192), bf16),
            pltpu.VMEM((16, 8192), f32),
            pltpu.VMEM((144, 8192), bf16),
            pltpu.VMEM((8448, 128), bf16),
            pltpu.VMEM((8448, 128), bf16),
            pltpu.VMEM((72, 8192), f32),
            pltpu.VMEM((2, 64, 128), f32),
            pltpu.VMEM((64, 2, 128), f32),
            pltpu.VMEM((64, 2, 128), f32),
            pltpu.VMEM((64, 4, 128), f32),
            pltpu.VMEM((64, 4, 128), f32),
            pltpu.VMEM((16, 256), bf16),
            pltpu.VMEM((8, 16, 256), bf16),
            pltpu.VMEM((256, 128), f32),
            pltpu.VMEM((2, 4, 2, 2, 4, 32, 256), bf16),
            pltpu.VMEM((4, 2, 2, 256, 256), bf16),
            pltpu.VMEM((2, 4, 8, 64, 256), bf16),
            pltpu.VMEM((3, 3, 2, 64, 128), jnp.int16),
            pltpu.VMEM((3, 3, 2, 128), f32),
            pltpu.VMEM((3, 3, 2, 64, 128), jnp.int16),
            pltpu.VMEM((3, 3, 2, 128), f32),
            pltpu.VMEM((2, 2, 64, 128), jnp.int16),
            pltpu.VMEM((2, 2, 128), f32),
            pltpu.VMEM((2, 4, 2, 64, 128), jnp.int16),
            pltpu.VMEM((2, 4, 2, 128), f32),
            pltpu.VMEM((2, 32, 2, 128), f32),
            pltpu.VMEM((2, 8, 2, 128), f32),
            pltpu.VMEM((2, 2, 2, 128), f32),
            dma((22,)),
            dma((3, 3, 2)),
            dma((2, 3, 2)),
            dma((7,)),
            dma((2,)),
            dma((2,)),
            dma((2, 7)),
            dma((6,)),
            dma((6,)),
            dma((4,)),
            dma((4,)),
            dma((2,)),
        ],
        compiler_params=pltpu.CompilerParams(
            collective_id=0, has_side_effects=True, vmem_limit_bytes=60 * 1024 * 1024
        ),
    )(
        prior_image[0],
        spectrum,
        maps,
        sampling,
        w1,
        w2,
        w3,
        b1,
        b2,
        bias_last,
        jnp.asarray(forward),
        jnp.asarray(backward),
        jnp.asarray(z_forward),
        jnp.asarray(z_backward),
    )
    return out[0:1], out[1:2]


def solution(mesh):
    torus = Mesh(mesh.devices.reshape(SIZES), AXES)
    coil = ("y", "g", "b")
    slab = ("x", "k")
    in_specs = (
        P(ALL, None, None),
        P(coil, slab, None, None),
        P(coil, slab, None, None),
        P(slab, None),
        P(),
        P(),
        P(),
        P(),
        P(),
        P(),
    )
    out_specs = (P(ALL, None, None), P(ALL, None, None))
    return jax.shard_map(body, mesh=torus, in_specs=in_specs, out_specs=out_specs, check_vma=False)
```

```python
import functools

import jax
import jax.numpy as jnp
import numpy as np
from jax import lax
from jax.experimental import pallas as pl
from jax.experimental.pallas import tpu as pltpu
from jax.sharding import Mesh
from jax.sharding import PartitionSpec as P

AXES = ("x", "k", "y", "g", "b")
SIZES = (4, 2, 4, 4, 2)
GROUP = ("x", "k", "y", "b")
ALL = ("x", "k", "y", "g", "b")

penalty = 0.5
f32 = jnp.float32
bf16 = jnp.bfloat16


def split_table(table):
    table = table.astype(np.float32)
    high = table.astype(jnp.bfloat16)
    low = (table - high.astype(np.float32)).astype(jnp.bfloat16)
    return np.stack([high, low])


def row_order():
    order = np.zeros(256, np.int64)
    for g in range(4):
        for s in range(8):
            for y in range(4):
                for b in range(2):
                    order[g * 64 + s * 8 + y * 2 + b] = s * 32 + y * 8 + 2 * g + b
    return order


def tables():
    rows = row_order().reshape(4, 2, 32)[:, 0].reshape(128)
    forward, backward = [], []
    for parity in range(2):
        angle = 2 * np.pi * (np.outer(2 * np.arange(128) + parity, rows) % 256) / 256
        c, s = np.cos(angle) / 16.0, np.sin(angle) / 16.0
        forward.append(split_table(np.block([[c, s], [-s, c]])))
        backward.append(split_table(np.block([[c.T, -s.T], [s.T, c.T]])))
    angle = 2 * np.pi * (np.outer(np.arange(128), np.arange(128)) % 128) / 128
    c, s = np.cos(angle) / np.sqrt(128.0), np.sin(angle) / np.sqrt(128.0)
    z_forward = split_table(np.block([[c, -s], [s, c]]))
    z_backward = split_table(np.block([[c, s], [-s, c]]))
    return np.stack(forward), np.stack(backward), z_forward, z_backward


def halves(value):
    high = value.astype(bf16)
    low = (value - high.astype(f32)).astype(bf16)
    return high, low


def mm(a, b):
    return jnp.dot(a, b, preferred_element_type=f32)


def three(left, right):
    return mm(left[0], right[0]) + (mm(left[0], right[1]) + mm(left[1], right[0]))


def coded(value):
    peak = jnp.maximum(jnp.max(jnp.abs(value), axis=1, keepdims=True), 1e-30)
    code = jnp.round(value * (32767.0 / peak)).astype(jnp.int32).astype(jnp.int16)
    return code, peak[:, 0]


def decoded(code, peak):
    return code.astype(jnp.int32).astype(f32) * (peak * (1.0 / 32767.0))[:, None]


def folded(value):
    return value.reshape(-1, 8, 128).sum(axis=0)


def decode_all(i):
    return {
        "x": i // 64,
        "k": lax.rem(i // 32, 2),
        "y": lax.rem(i // 8, 4),
        "g": lax.rem(i // 2, 4),
        "b": lax.rem(i, 2),
    }


def lanes(shape):
    return lax.broadcasted_iota(jnp.int32, shape, len(shape) - 1)


def plane_shift(value, dz):
    if dz == 0:
        return value
    if dz < 0:
        edge = pltpu.roll(value[:, -128:], 64, 1)
        edge = jnp.where(lanes(edge.shape) >= 64, edge, 0.0)
        return jnp.concatenate([edge, value[:, :-128]], axis=1)
    edge = pltpu.roll(value[:, :128], 64, 1)
    edge = jnp.where(lanes(edge.shape) < 64, edge, 0.0)
    return jnp.concatenate([value[:, 128:], edge], axis=1)


def column_shift(value, dx):
    if dx == 0:
        return value
    width = value.shape[1]
    column = lax.rem(lanes(value.shape), 64)
    if dx < 0:
        return jnp.where(column != 0, pltpu.roll(value, 1, 1), 0.0)
    return jnp.where(column != 63, pltpu.roll(value, width - 1, 1), 0.0)


def step_kernel(
    prior_ref,
    k_hbm,
    m_hbm,
    sampling_ref,
    first_ref,
    middle_ref,
    last_ref,
    b1_ref,
    b2_ref,
    b3_ref,
    fy_hbm,
    gy_hbm,
    fz_hbm,
    gz_hbm,
    out_ref,
    fy_ref,
    gy_ref,
    fz_ref,
    gz_ref,
    w1_wide,
    w1_ref,
    w2_turned,
    w2_ref,
    w3_wide,
    w3_ref,
    k_ref,
    m_ref,
    s_ref,
    cells,
    flat,
    feat,
    fbuf,
    f_rows,
    a1,
    h1m,
    h1e,
    p3,
    dplanes,
    dsrc,
    dbuf,
    osrc,
    obuf,
    mask_own,
    mask_all,
    mask_t,
    rows_in,
    spectra,
    rows_out,
    out_code,
    out_peak,
    part_code,
    part_peak,
    own_code,
    own_peak,
    full_code,
    full_peak,
    stat_a,
    stat_c,
    stat_own,
    send_sem,
    part_sem,
    full_sem,
    mask_sem,
    stat_send,
    stat_sem_a,
    stat_sem_c,
    feat_send,
    feat_sem,
    bulk_send,
    bulk_sem,
    local_sem,
):
    x, k, y, g, b = (lax.axis_index(name) for name in AXES)
    slab = x * 2 + k
    line = g * 2 + b
    me = x * 16 + k * 8 + y * 2 + b
    row = slab * 32 + y * 8 + line

    xs = [lax.rem(x + i, 4) for i in range(4)]
    ks = [k, 1 - k]
    ys = [lax.rem(y + i, 4) for i in range(4)]
    bs = [b, 1 - b]
    group = []
    for n in range(64):
        i, j = n % 4, n // 4 % 4
        offset = (i, (n // 16 + j) % 2, (i + j) % 4, (n // 32 + i) % 2)
        if any(offset):
            there = xs[offset[0]], ks[offset[1]], ys[offset[2]], bs[offset[3]]
            index = there[0] * 16 + there[1] * 8 + there[2] * 2 + there[3]
            group.append((index, dict(zip(GROUP, there))))

    def row_peer(i):
        return decode_all(lax.rem(row + 256 + i, 256))

    def slab_peer(i):
        t = lax.rem(slab + i, 8)
        return t, {"x": t // 2, "k": lax.rem(t, 2)}

    def line_peer(i):
        t = lax.rem(line + i, 8)
        return t, {"g": t // 2, "b": lax.rem(t, 2)}

    def g_peer(i):
        t = lax.rem(g + i, 4)
        return t, {"g": t}

    mesh_id = pl.DeviceIdType.MESH
    barrier = pltpu.get_barrier_semaphore()

    for _, device in group:
        pl.semaphore_signal(barrier, inc=1, device_id=device, device_id_type=mesh_id)
    for i in (-3, -2, -1, 1, 2, 3):
        pl.semaphore_signal(barrier, inc=1, device_id=row_peer(i), device_id_type=mesh_id)
    for i in range(1, 4):
        for c in range(2):
            pl.semaphore_signal(
                barrier,
                inc=1,
                device_id={"g": lax.rem(g + i, 4), "b": lax.rem(b + c, 2)},
                device_id_type=mesh_id,
            )
    table_copies = []
    for n, (source, target) in enumerate(
        ((fy_hbm, fy_ref), (gy_hbm, gy_ref), (fz_hbm, fz_ref), (gz_hbm, gz_ref))
    ):
        table_copies.append(pltpu.make_async_copy(source, target, local_sem.at[2 + n]))
        table_copies[n].start()
    w1_wide[...] = jnp.zeros_like(w1_wide)
    w2_turned[...] = jnp.zeros_like(w2_turned)
    w3_wide[...] = jnp.zeros_like(w3_wide)
    for a in range(3):
        for tap in range(9):
            dz, dx = tap // 3, tap % 3
            value = first_ref[9 * a + tap].astype(f32)
            for r in range(7):
                place = 16 * tap + 2 * (min(r, 4) + a)
                w1_wide[place : place + 2, 32 * r : 32 * r + 32] = value
            w3_wide[8 * tap : 8 * tap + 2, 32 * a : 32 * a + 32] = last_ref[9 * a + tap].astype(f32)
            value = middle_ref[9 * a + tap]
            for r in range(3):
                place = 128 * dz + 32 * (r + a) if r + a < 4 else 384 + 32 * dz
                w2_turned[128 * dx + 32 * r : 128 * dx + 32 * r + 32, place : place + 32] = value
    w1_ref[...] = w1_wide[...].astype(bf16)
    w2_ref[...] = jnp.transpose(w2_turned[...].astype(f32)).astype(bf16)
    w3_ref[...] = w3_wide[...].astype(bf16)
    mask_own[...] = sampling_ref[...].astype(f32).astype(bf16)
    left = lanes((64, 128)) < 64
    top, bottom = prior_ref[0:64], prior_ref[64:128]
    cells[0] = jnp.where(left, top, pltpu.roll(bottom, 64, 1))
    cells[1] = jnp.where(left, pltpu.roll(top, 64, 1), bottom)
    for i in range(64):
        for c in range(2):
            flat[c : c + 1, 128 * i : 128 * i + 128] = cells[c, i : i + 1]
    feat[...] = flat[...].astype(bf16)
    k_local = pltpu.make_async_copy(k_hbm.at[me], k_ref.at[me], local_sem.at[0])
    m_local = pltpu.make_async_copy(m_hbm.at[me], m_ref.at[me], local_sem.at[1])
    k_local.start()
    m_local.start()
    pl.semaphore_wait(barrier, 75)

    def copy_to(source, target, departure, arrival, device):
        copy = pltpu.make_async_remote_copy(
            src_ref=source,
            dst_ref=target,
            send_sem=departure,
            recv_sem=arrival,
            device_id=device,
            device_id_type=mesh_id,
        )
        copy.start()
        return copy

    def send(source, target, slot, arrival, device):
        return copy_to(source, target, send_sem.at[slot], arrival, device)

    def bulk(*jobs):
        for t, device in group:
            for which, source, target in jobs:
                copy_to(
                    source.at[t], target.at[me], bulk_send.at[which], bulk_sem.at[which], device
                )

    def bulk_wait(which, source, target):
        pltpu.make_async_copy(
            target.at[pl.ds(0, 63)], target.at[pl.ds(0, 63)], bulk_sem.at[which]
        ).wait()
        pltpu.make_async_copy(
            source.at[pl.ds(0, 63)], source.at[pl.ds(0, 63)], bulk_send.at[which]
        ).wait()

    feat_copies = []
    for n, i in enumerate((-1, 1, -2, 2, -3, 3)):
        feat_copies.append(
            copy_to(feat, fbuf.at[3 - i], feat_send.at[n], feat_sem.at[n], row_peer(i))
        )
    mask_copies = []
    for i in range(1, 8):
        mask_copies.append(
            send(mask_own, mask_all.at[slab], i - 1, mask_sem.at[i - 1], slab_peer(i)[1])
        )
    mask_all[pl.ds(slab, 1)] = mask_own[...][None]
    bulk((0, k_hbm, k_ref))
    bulk((1, m_hbm, m_ref))

    fbuf[3] = feat[...]
    for copy in feat_copies:
        copy.wait()
    f_rows[14:16] = jnp.zeros((2, 8192), f32)
    for r in range(7):
        inside = jnp.logical_and(row + r >= 3, row + r < 259)
        f_rows[2 * r : 2 * r + 2] = jnp.where(inside, fbuf[r].astype(f32), 0.0)
    for dx in range(3):
        shifted = column_shift(f_rows[...], dx - 1)
        for dz in range(3):
            tap = dz * 3 + dx
            a1[16 * tap : 16 * tap + 16] = plane_shift(shifted, dz - 1).astype(bf16)

    bias_one = jnp.concatenate([b1_ref[...]] * 8, axis=1)
    bias_two = jnp.concatenate([b2_ref[...]] * 4, axis=1)
    lane = lanes((1, 256))
    hidden_row = row - 2 + jnp.minimum(lane // 32, 4)
    keep1 = jnp.where(jnp.logical_and(hidden_row >= 0, hidden_row < 256), 1.0, 0.0)
    lane = lanes((1, 128))
    hidden_row = row - 1 + jnp.minimum(lane // 32, 2)
    keep2 = jnp.where(jnp.logical_and(hidden_row >= 0, hidden_row < 256), 1.0, 0.0)
    h1e[...] = jnp.zeros_like(h1e)

    def layer_one(n, _):
        first = pl.multiple_of(n * 512, 512)
        block = lax.dot_general(
            a1[:, pl.ds(first, 512)],
            w1_ref[...],
            (((0,), (0,)), ((), ())),
            preferred_element_type=f32,
        )
        block = (jnp.maximum(block + bias_one, 0.0) * keep1).astype(bf16)
        h1m[pl.ds(pl.multiple_of(first + 128, 128), 512)] = block[:, :128]
        for dz in range(3):
            h1e[pl.ds(pl.multiple_of(first + 256 - 128 * dz, 128), 512), 32 * dz : 32 * dz + 32] = (
                block[:, 128 + 32 * dz : 160 + 32 * dz]
            )
        return 0

    lax.fori_loop(0, 16, layer_one, 0)
    zero = jnp.zeros((64, 128), bf16)
    h1m[0:64] = zero
    h1m[64:128] = h1m[128 + 8064 : 128 + 8128]
    h1m[128 + 8192 : 128 + 8256] = h1m[192:256]
    h1m[128 + 8256 : 128 + 8320] = zero
    h1e[128:192, 0:32] = jnp.zeros((64, 32), bf16)
    h1e[192:256, 0:32] = h1e[128 + 8064 : 128 + 8128, 32:64]
    return_rows = h1e[192:256, 32:64]
    h1e[128 + 8064 : 128 + 8128, 64:96] = return_rows
    h1e[128 + 8128 : 128 + 8192, 64:96] = jnp.zeros((64, 32), bf16)

    def layer_two(n, _):
        first = pl.multiple_of(n * 512, 512)
        low = jnp.concatenate(
            [
                h1m[pl.ds(first, 512)],
                h1m[pl.ds(pl.multiple_of(first + 128, 128), 512)],
                h1m[pl.ds(pl.multiple_of(first + 256, 128), 512)],
                h1e[pl.ds(pl.multiple_of(first + 128, 128), 512)],
            ],
            axis=1,
        )
        block = mm(low, w2_ref[...])
        column = lax.rem(lax.broadcasted_iota(jnp.int32, (512, 128), 0), 64)
        block = (
            jnp.where(column != 0, pltpu.roll(block[:, :128], 1, 0), 0.0)
            + block[:, 128:256]
            + jnp.where(column != 63, pltpu.roll(block[:, 256:], 511, 0), 0.0)
        )
        block = (jnp.maximum(block + bias_two, 0.0) * keep2).astype(bf16)
        p3[:, pl.ds(first, 512)] = lax.dot_general(
            w3_ref[...], block, (((1,), (1,)), ((), ())), preferred_element_type=f32
        )
        return 0

    lax.fori_loop(0, 16, layer_two, 0)
    total = jnp.zeros((8, 8192), f32)
    for dx in range(3):
        side = jnp.zeros((8, 8192), f32)
        for dz in range(3):
            tap = dz * 3 + dx
            side = side + plane_shift(p3[8 * tap : 8 * tap + 8], dz - 1)
        total = total + column_shift(side, dx - 1)
    for i in range(64):
        for c in range(2):
            dplanes[c, i : i + 1] = total[c : c + 1, 128 * i : 128 * i + 128]
    for c in range(2):
        turned = jnp.transpose(dplanes[c] + (cells[c] + b3_ref[c]))
        dsrc[:, c] = jnp.concatenate([turned[:64], turned[64:]], axis=1)
    bulk((2, dsrc, dbuf))
    dbuf[pl.ds(me, 1)] = dsrc[pl.ds(me, 1)]

    k_local.wait()
    for copy in table_copies:
        copy.wait()
    for copy in mask_copies:
        copy.wait()
    order = lax.broadcasted_iota(jnp.int32, (256, 256), 0)
    order = 2 * lax.rem(order, 128) + order // 128
    order = (order == lax.broadcasted_iota(jnp.int32, (256, 256), 1)).astype(bf16)
    mask_rows = mask_all[...].reshape(128, 256)
    by_line = (((1,), (1,)), ((), ()))
    mask_t[...] = lax.dot_general(order, mask_rows, by_line, preferred_element_type=f32)
    bulk_wait(0, k_hbm, k_ref)

    def put_rows(pair, even, odd):
        for h, part in ((0, even + odd), (1, even - odd)):
            for q, value in enumerate(halves(part)):
                for n in range(2):
                    first = slice(128 * n, 128 * n + 128)
                    piece = jnp.concatenate([value[:128, first], value[128:, first]], axis=1)
                    for i in range(4):
                        rows_out[q, i, 2 * pair + n, 32 * h : 32 * h + 32] = piece[
                            32 * i : 32 * i + 32
                        ]

    def adjoint_pair(pair, _):
        planes = []
        for n in range(2):
            for c in range(2):
                plane = jnp.concatenate(
                    [k_ref[8 * s + 2 * pair + n, c] for s in range(8)], axis=0
                )
                planes.append(plane * mask_rows)
        planes = lax.dot_general(
            jnp.concatenate(planes, axis=0), order, by_line, preferred_element_type=f32
        ).astype(bf16)
        sides = []
        for p in range(2):
            cell = slice(128 * p, 128 * p + 128)
            spectrum = jnp.concatenate(
                [
                    jnp.concatenate([planes[0:128, cell], planes[128:256, cell]], axis=1),
                    jnp.concatenate([planes[256:384, cell], planes[384:512, cell]], axis=1),
                ],
                axis=0,
            )
            sides.append(
                lax.dot_general(gy_ref[p, 0], spectrum, by_line, preferred_element_type=f32)
                + lax.dot_general(gy_ref[p, 1], spectrum, by_line, preferred_element_type=f32)
            )
        put_rows(pair, *sides)
        return 0

    lax.fori_loop(0, 4, adjoint_pair, 0, unroll=2)
    m_local.wait()
    bulk_wait(1, m_hbm, m_ref)

    def widen_maps(j, _):
        for c in range(2):
            for h in range(4):
                for s in range(8):
                    first = h * 64 + s * 8
                    s_ref[j, c, first : first + 8] = m_ref[8 * s + j, c, h].astype(f32)
        return 0

    lax.fori_loop(0, 8, widen_maps, 0, unroll=2)

    def maps_of(j, h):
        rows = pl.ds(pl.multiple_of(h * 64, 64), 64)
        return s_ref[j, 0, rows], s_ref[j, 1, rows]

    def image_rows(h):
        left = rows_out[0, h].reshape(512, 256), rows_out[1, h].reshape(512, 256)
        image = three(left, (gz_ref[0], gz_ref[1]))
        real_total, imag_total = 0.0, 0.0
        for j in range(8):
            real, imag = maps_of(j, h)
            a_real = image[64 * j : 64 * j + 64, :128]
            a_imag = image[64 * j : 64 * j + 64, 128:]
            real_total = real_total + (real * a_real + imag * a_imag)
            imag_total = imag_total + (real * a_imag - imag * a_real)
        return jnp.stack([real_total, imag_total])

    def reduce_scatter(step, between=lambda: None):
        copies = []
        for i in (2, 1, 3):
            t, device = g_peer(i)
            code, peak = coded(image_rows(t))
            out_code[step, i - 1] = code
            out_peak[step, i - 1] = peak
            for n, (source, target) in enumerate(((out_code, part_code), (out_peak, part_peak))):
                copies.append(
                    send(
                        source.at[step, i - 1],
                        target.at[step, i - 1],
                        13 + 2 * i + n,
                        part_sem.at[step, i - 1, n],
                        device,
                    )
                )
        between()
        total = image_rows(g)

        def finish():
            for copy in copies:
                copy.wait()
            value = total
            for i in range(3):
                value = value + decoded(part_code[step, i], part_peak[step, i])
            return value

        return finish

    def gather(step, value):
        code, peak = coded(value)
        own_code[step] = code
        own_peak[step] = peak
        copies = {}
        for i in (2, 1, 3):
            _, device = g_peer(i)
            copies[i] = [
                send(
                    source.at[step],
                    target.at[step, g],
                    13 + 2 * i + n,
                    full_sem.at[step, i - 1, n],
                    device,
                )
                for n, (source, target) in enumerate(((own_code, full_code), (own_peak, full_peak)))
            ]

        def finish(i):
            for copy in copies[i]:
                copy.wait()
            t = lax.rem(g + 4 - i, 4)
            return t, decoded(full_code[step, t], full_peak[step, t])

        return finish

    def forward_rows(h, value):
        pieces = []
        for j in range(8):
            real, imag = maps_of(j, h)
            pieces.append(
                jnp.concatenate(
                    [
                        real * value[0] - imag * value[1],
                        real * value[1] + imag * value[0],
                    ],
                    axis=1,
                )
            )
        lines = three(halves(jnp.concatenate(pieces, axis=0)), (fz_ref[0], fz_ref[1]))
        for j in range(8):
            low, high = lines[64 * j : 64 * j + 32], lines[64 * j + 32 : 64 * j + 64]
            place = slice(128 * (j % 2), 128 * (j % 2) + 128)
            for p, part in enumerate((low + high, low - high)):
                for q, piece in enumerate(halves(part)):
                    for c in range(2):
                        rows_in[q, j // 2, p, c, h, :, place] = piece[:, 128 * c : 128 * c + 128]

    def forward_pair(pair, energy):
        for p in range(2):
            mask = mask_t[128 * p : 128 * p + 128]
            mask = jnp.concatenate([mask, mask], axis=1)
            mask = jnp.concatenate([mask, mask], axis=0)
            sides = [rows_in[q, pair, p].reshape(256, 256) for q in range(2)]
            spectrum = three((fy_ref[p, 0], fy_ref[p, 1]), sides) * mask
            squares = spectrum * spectrum
            energy = energy + folded(squares[:, :128] + squares[:, 128:])
            high, low = halves(spectrum)
            spectra[pair, p, 0] = high
            spectra[pair, p, 1] = low
        return energy

    def inverse_pair(pair, _):
        sides = []
        for p in range(2):
            right = spectra[pair, p, 0], spectra[pair, p, 1]
            sides.append(three((gy_ref[p, 0], gy_ref[p, 1]), right))
        put_rows(pair, *sides)
        return 0

    here = x * 8 + k * 4 + y
    plane = [
        {"x": xs[i], "k": ks[j], "y": ys[n]}
        for n in range(4)
        for j in range(2)
        for i in range(4)
        if i or j or n
    ]

    def plane_total(step, value):
        stat_own[step, 0] = value
        stat_a[step, pl.ds(here, 1)] = value[None]
        for device in plane:
            copy_to(
                stat_own.at[step, 0],
                stat_a.at[step, here],
                stat_send.at[step],
                stat_sem_a.at[step],
                device,
            )

        def finish():
            block = stat_a.at[step, pl.ds(0, 31)]
            pltpu.make_async_copy(block, block, stat_sem_a.at[step]).wait()
            pltpu.make_async_copy(block, block, stat_send.at[step]).wait()
            value = stat_a[step, 0]
            for i in range(1, 32):
                value = value + stat_a[step, i]
            return value

        return finish

    def line_total(step, value):
        stat_own[step, 1] = value
        stat_c[step, pl.ds(line, 1)] = value[None]
        copies = []
        for i in range(1, 8):
            copies.append(
                send(
                    stat_own.at[step, 1],
                    stat_c.at[step, line],
                    7 + i,
                    stat_sem_c.at[step, i - 1],
                    line_peer(i)[1],
                )
            )

        def finish():
            for copy in copies:
                copy.wait()
            value = stat_c[step, 0]
            for i in range(1, 8):
                value = value + stat_c[step, i]
            return value

        return finish

    def norm_of(value):
        return folded((value * value).reshape(128, 128))

    def operator(step, direction):
        finish = gather(step, direction)
        norm = norm_of(direction)
        forward_rows(g, direction)
        for i in (1, 3, 2):
            forward_rows(*finish(i))
        energy = lax.fori_loop(0, 4, forward_pair, jnp.zeros((8, 128), f32), unroll=2)
        stats = [jnp.sum(value, axis=0, keepdims=True) for value in (norm, energy)]
        finish_plane = plane_total(step, jnp.concatenate(stats, axis=0))
        lax.fori_loop(0, 4, inverse_pair, 0, unroll=2)
        last = []
        image = reduce_scatter(
            step + 1, lambda: last.append(line_total(step, finish_plane()))
        )
        value = last[0]()
        norm, energy = jnp.sum(value[0:1]), jnp.sum(value[1:2])
        return norm, energy + penalty * norm, image() + penalty * direction

    right = reduce_scatter(0)()
    bulk_wait(2, dsrc, dbuf)
    right = right + penalty * jnp.stack([dbuf[:, 0], dbuf[:, 1]])
    rr, curvature, image = operator(0, right)
    alpha = rr / curvature
    residual = right - alpha * image
    fresh, curvature, second = operator(1, residual)
    growth = fresh / rr
    step_size = fresh / (curvature - growth * fresh / alpha)
    q = second + growth * image
    answer = alpha * right + step_size * (residual + growth * right)
    rest = residual - step_size * q
    for c in range(2):
        osrc[:, c] = answer[c]
        osrc[:, 2 + c] = rest[c]
    bulk((3, osrc, obuf))
    obuf[pl.ds(me, 1)] = osrc[pl.ds(me, 1)]
    bulk_wait(3, osrc, obuf)
    out_ref[0] = jnp.transpose(jnp.concatenate([obuf[:, 0], obuf[:, 1]], axis=0))
    out_ref[1] = jnp.transpose(jnp.concatenate([obuf[:, 2], obuf[:, 3]], axis=0))


def body(
    prior_image,
    coil_maps,
    kspace,
    sampling,
    weight_first,
    bias_first,
    weight_middle,
    bias_middle,
    weight_last,
    bias_last,
):
    spectrum = kspace[0].reshape(16, 256, 2, 64).transpose(3, 2, 0, 1)
    maps = coil_maps[0].reshape(4, 4, 2, 128, 2, 64).transpose(5, 4, 1, 0, 2, 3)
    maps = maps.reshape(64, 2, 4, 8, 128)

    b1 = bias_first[None]
    b2 = bias_middle[None]

    forward, backward, z_forward, z_backward = tables()
    vmem = pl.BlockSpec(memory_space=pltpu.VMEM)
    hbm = pl.BlockSpec(memory_space=pl.ANY)
    out = jax.ShapeDtypeStruct((2, 128, 128), f32)
    smem = pl.BlockSpec(memory_space=pltpu.SMEM)
    dma = pltpu.SemaphoreType.DMA
    out = pl.pallas_call(
        step_kernel,
        out_shape=out,
        in_specs=[vmem] + [hbm] * 2 + [vmem] * 6 + [smem] + [hbm] * 4,
        out_specs=vmem,
        scratch_shapes=[
            pltpu.VMEM((2, 2, 256, 256), bf16),
            pltpu.VMEM((2, 2, 256, 256), bf16),
            pltpu.VMEM((2, 256, 256), bf16),
            pltpu.VMEM((2, 256, 256), bf16),
            pltpu.VMEM((144, 256), f32),
            pltpu.VMEM((144, 256), bf16),
            pltpu.VMEM((384, 512), bf16),
            pltpu.VMEM((512, 384), bf16),
            pltpu.VMEM((72, 128), f32),
            pltpu.VMEM((72, 128), bf16),
            pltpu.VMEM((64, 2, 16, 256), bf16),
            pltpu.VMEM((64, 2, 4, 8, 128), bf16),
            pltpu.VMEM((8, 2, 256, 128), f32),
            pltpu.VMEM((2, 64, 128), f32),
            pltpu.VMEM((2, 8192), f32),
            pltpu.VMEM((2, 8192), bf16),
            pltpu.VMEM((7, 2, 8192), bf16),
            pltpu.VMEM((16, 8192), f32),
            pltpu.VMEM((144, 8192), bf16),
            pltpu.VMEM((8448, 128), bf16),
            pltpu.VMEM((8448, 128), bf16),
            pltpu.VMEM((72, 8192), f32),
            pltpu.VMEM((2, 64, 128), f32),
            pltpu.VMEM((64, 2, 128), f32),
            pltpu.VMEM((64, 2, 128), f32),
            pltpu.VMEM((64, 4, 128), f32),
            pltpu.VMEM((64, 4, 128), f32),
            pltpu.VMEM((16, 256), bf16),
            pltpu.VMEM((8, 16, 256), bf16),
            pltpu.VMEM((256, 128), f32),
            pltpu.VMEM((2, 4, 2, 2, 4, 32, 256), bf16),
            pltpu.VMEM((4, 2, 2, 256, 256), bf16),
            pltpu.VMEM((2, 4, 8, 64, 256), bf16),
            pltpu.VMEM((3, 3, 2, 64, 128), jnp.int16),
            pltpu.VMEM((3, 3, 2, 128), f32),
            pltpu.VMEM((3, 3, 2, 64, 128), jnp.int16),
            pltpu.VMEM((3, 3, 2, 128), f32),
            pltpu.VMEM((2, 2, 64, 128), jnp.int16),
            pltpu.VMEM((2, 2, 128), f32),
            pltpu.VMEM((2, 4, 2, 64, 128), jnp.int16),
            pltpu.VMEM((2, 4, 2, 128), f32),
            pltpu.VMEM((2, 32, 2, 128), f32),
            pltpu.VMEM((2, 8, 2, 128), f32),
            pltpu.VMEM((2, 2, 2, 128), f32),
            dma((22,)),
            dma((3, 3, 2)),
            dma((2, 3, 2)),
            dma((7,)),
            dma((2,)),
            dma((2,)),
            dma((2, 7)),
            dma((6,)),
            dma((6,)),
            dma((4,)),
            dma((4,)),
            dma((6,)),
        ],
        compiler_params=pltpu.CompilerParams(
            collective_id=0, has_side_effects=True, vmem_limit_bytes=60 * 1024 * 1024
        ),
    )(
        prior_image[0],
        spectrum,
        maps,
        sampling,
        weight_first.transpose(0, 1, 2, 4, 3).reshape(27, 2, 32),
        weight_middle.reshape(27, 32, 32),
        weight_last.reshape(27, 2, 32),
        b1,
        b2,
        bias_last,
        jnp.asarray(forward),
        jnp.asarray(backward),
        jnp.asarray(z_forward),
        jnp.asarray(z_backward),
    )
    return out[0:1], out[1:2]


def solution(mesh):
    torus = Mesh(mesh.devices.reshape(SIZES), AXES)
    coil = ("y", "g", "b")
    slab = ("x", "k")
    in_specs = (
        P(ALL, None, None),
        P(coil, slab, None, None),
        P(coil, slab, None, None),
        P(slab, None),
        P(),
        P(),
        P(),
        P(),
        P(),
        P(),
    )
    out_specs = (P(ALL, None, None), P(ALL, None, None))
    return jax.shard_map(body, mesh=torus, in_specs=in_specs, out_specs=out_specs, check_vma=False)
```

```python
import functools

import jax
import jax.numpy as jnp
import numpy as np
from jax import lax
from jax.experimental import pallas as pl
from jax.experimental.pallas import tpu as pltpu
from jax.sharding import Mesh
from jax.sharding import PartitionSpec as P

AXES = ("x", "k", "y", "g", "b")
SIZES = (4, 2, 4, 4, 2)
GROUP = ("x", "k", "y", "b")
ALL = ("x", "k", "y", "g", "b")

penalty = 0.5
f32 = jnp.float32
bf16 = jnp.bfloat16


def split_table(table):
    table = table.astype(np.float32)
    high = table.astype(jnp.bfloat16)
    low = (table - high.astype(np.float32)).astype(jnp.bfloat16)
    return np.stack([high, low])


def row_order():
    order = np.zeros(256, np.int64)
    for g in range(4):
        for s in range(8):
            for y in range(4):
                for b in range(2):
                    order[g * 64 + s * 8 + y * 2 + b] = s * 32 + y * 8 + 2 * g + b
    return order


def tables():
    rows = row_order().reshape(4, 2, 32)[:, 0].reshape(128)
    forward, backward = [], []
    for parity in range(2):
        angle = 2 * np.pi * (np.outer(2 * np.arange(128) + parity, rows) % 256) / 256
        c, s = np.cos(angle) / 16.0, np.sin(angle) / 16.0
        forward.append(split_table(np.block([[c, s], [-s, c]])))
        backward.append(split_table(np.block([[c.T, -s.T], [s.T, c.T]])))
    angle = 2 * np.pi * (np.outer(np.arange(128), np.arange(128)) % 128) / 128
    c, s = np.cos(angle) / np.sqrt(128.0), np.sin(angle) / np.sqrt(128.0)
    z_forward = split_table(np.block([[c, -s], [s, c]]))
    z_backward = split_table(np.block([[c, s], [-s, c]]))
    return np.stack(forward), np.stack(backward), z_forward, z_backward


def halves(value):
    high = value.astype(bf16)
    low = (value - high.astype(f32)).astype(bf16)
    return high, low


def mm(a, b):
    return jnp.dot(a, b, preferred_element_type=f32)


def three(left, right):
    return mm(left[0], right[0]) + (mm(left[0], right[1]) + mm(left[1], right[0]))


def coded(value):
    peak = jnp.maximum(jnp.max(jnp.abs(value), axis=1, keepdims=True), 1e-30)
    code = jnp.round(value * (32767.0 / peak)).astype(jnp.int32).astype(jnp.int16)
    return code, peak[:, 0]


def decoded(code, peak):
    return code.astype(jnp.int32).astype(f32) * (peak * (1.0 / 32767.0))[:, None]


def folded(value):
    return value.reshape(-1, 8, 128).sum(axis=0)


def decode_all(i):
    return {
        "x": i // 64,
        "k": lax.rem(i // 32, 2),
        "y": lax.rem(i // 8, 4),
        "g": lax.rem(i // 2, 4),
        "b": lax.rem(i, 2),
    }


def lanes(shape):
    return lax.broadcasted_iota(jnp.int32, shape, len(shape) - 1)


def plane_shift(value, dz):
    if dz == 0:
        return value
    if dz < 0:
        edge = pltpu.roll(value[:, -128:], 64, 1)
        edge = jnp.where(lanes(edge.shape) >= 64, edge, 0.0)
        return jnp.concatenate([edge, value[:, :-128]], axis=1)
    edge = pltpu.roll(value[:, :128], 64, 1)
    edge = jnp.where(lanes(edge.shape) < 64, edge, 0.0)
    return jnp.concatenate([value[:, 128:], edge], axis=1)


def column_shift(value, dx):
    if dx == 0:
        return value
    width = value.shape[1]
    column = lax.rem(lanes(value.shape), 64)
    if dx < 0:
        return jnp.where(column != 0, pltpu.roll(value, 1, 1), 0.0)
    return jnp.where(column != 63, pltpu.roll(value, width - 1, 1), 0.0)


def step_kernel(
    prior_ref,
    k_hbm,
    m_hbm,
    sampling_ref,
    first_ref,
    middle_ref,
    last_ref,
    b1_ref,
    b2_ref,
    b3_ref,
    fy_hbm,
    gy_hbm,
    fz_hbm,
    gz_hbm,
    out_ref,
    fy_ref,
    gy_ref,
    fz_ref,
    gz_ref,
    w1_wide,
    w1_ref,
    w2_turned,
    w2_ref,
    w3_wide,
    w3_ref,
    k_ref,
    m_ref,
    s_ref,
    cells,
    flat,
    feat,
    fbuf,
    f_rows,
    a1,
    h1m,
    h1e,
    p3,
    dplanes,
    dsrc,
    dbuf,
    osrc,
    obuf,
    mask_own,
    mask_all,
    mask_t,
    rows_in,
    spectra,
    rows_out,
    out_code,
    out_peak,
    part_code,
    part_peak,
    own_code,
    own_peak,
    full_code,
    full_peak,
    stat_a,
    stat_c,
    stat_own,
    send_sem,
    part_sem,
    full_sem,
    mask_sem,
    stat_send,
    stat_sem_a,
    stat_sem_c,
    feat_send,
    feat_sem,
    bulk_send,
    bulk_sem,
    local_sem,
):
    x, k, y, g, b = (lax.axis_index(name) for name in AXES)
    slab = x * 2 + k
    line = g * 2 + b
    me = x * 16 + k * 8 + y * 2 + b
    row = slab * 32 + y * 8 + line

    xs = [lax.rem(x + i, 4) for i in range(4)]
    ks = [k, 1 - k]
    ys = [lax.rem(y + i, 4) for i in range(4)]
    bs = [b, 1 - b]
    group = []
    for n in range(64):
        i, j = n % 4, n // 4 % 4
        offset = (i, (n // 16 + j) % 2, (i + j) % 4, (n // 32 + i) % 2)
        if any(offset):
            there = xs[offset[0]], ks[offset[1]], ys[offset[2]], bs[offset[3]]
            index = there[0] * 16 + there[1] * 8 + there[2] * 2 + there[3]
            group.append((index, dict(zip(GROUP, there))))

    def row_peer(i):
        return decode_all(lax.rem(row + 256 + i, 256))

    def slab_peer(i):
        t = lax.rem(slab + i, 8)
        return t, {"x": t // 2, "k": lax.rem(t, 2)}

    def line_peer(i):
        t = lax.rem(line + i, 8)
        return t, {"g": t // 2, "b": lax.rem(t, 2)}

    def g_peer(i):
        t = lax.rem(g + i, 4)
        return t, {"g": t}

    mesh_id = pl.DeviceIdType.MESH
    barrier = pltpu.get_barrier_semaphore()

    for _, device in group:
        pl.semaphore_signal(barrier, inc=1, device_id=device, device_id_type=mesh_id)
    for i in (-3, -2, -1, 1, 2, 3):
        pl.semaphore_signal(barrier, inc=1, device_id=row_peer(i), device_id_type=mesh_id)
    for i in range(1, 4):
        for c in range(2):
            pl.semaphore_signal(
                barrier,
                inc=1,
                device_id={"g": lax.rem(g + i, 4), "b": lax.rem(b + c, 2)},
                device_id_type=mesh_id,
            )
    table_copies = []
    for n, (source, target) in enumerate(
        ((fy_hbm, fy_ref), (gy_hbm, gy_ref), (fz_hbm, fz_ref), (gz_hbm, gz_ref))
    ):
        table_copies.append(pltpu.make_async_copy(source, target, local_sem.at[2 + n]))
        table_copies[n].start()
    w1_wide[...] = jnp.zeros_like(w1_wide)
    w2_turned[...] = jnp.zeros_like(w2_turned)
    w3_wide[...] = jnp.zeros_like(w3_wide)
    for a in range(3):
        for tap in range(9):
            dz, dx = tap // 3, tap % 3
            value = first_ref[9 * a + tap].astype(f32)
            for r in range(7):
                place = 16 * tap + 2 * (min(r, 4) + a)
                w1_wide[place : place + 2, 32 * r : 32 * r + 32] = value
            w3_wide[8 * tap : 8 * tap + 2, 32 * a : 32 * a + 32] = last_ref[9 * a + tap].astype(f32)
            value = middle_ref[9 * a + tap]
            for r in range(3):
                place = 128 * dz + 32 * (r + a) if r + a < 4 else 384 + 32 * dz
                w2_turned[128 * dx + 32 * r : 128 * dx + 32 * r + 32, place : place + 32] = value
    w1_ref[...] = w1_wide[...].astype(bf16)
    w2_ref[...] = jnp.transpose(w2_turned[...].astype(f32)).astype(bf16)
    w3_ref[...] = w3_wide[...].astype(bf16)
    mask_own[...] = sampling_ref[...].astype(f32).astype(bf16)
    left = lanes((64, 128)) < 64
    top, bottom = prior_ref[0:64], prior_ref[64:128]
    cells[0] = jnp.where(left, top, pltpu.roll(bottom, 64, 1))
    cells[1] = jnp.where(left, pltpu.roll(top, 64, 1), bottom)
    for i in range(64):
        for c in range(2):
            flat[c : c + 1, 128 * i : 128 * i + 128] = cells[c, i : i + 1]
    feat[...] = flat[...].astype(bf16)
    k_local = pltpu.make_async_copy(k_hbm.at[me], k_ref.at[me], local_sem.at[0])
    m_local = pltpu.make_async_copy(m_hbm.at[me], m_ref.at[me], local_sem.at[1])
    k_local.start()
    m_local.start()
    pl.semaphore_wait(barrier, 75)

    def copy_to(source, target, departure, arrival, device):
        copy = pltpu.make_async_remote_copy(
            src_ref=source,
            dst_ref=target,
            send_sem=departure,
            recv_sem=arrival,
            device_id=device,
            device_id_type=mesh_id,
        )
        copy.start()
        return copy

    def send(source, target, slot, arrival, device):
        return copy_to(source, target, send_sem.at[slot], arrival, device)

    def bulk(*jobs):
        for t, device in group:
            for which, source, target in jobs:
                copy_to(
                    source.at[t], target.at[me], bulk_send.at[which], bulk_sem.at[which], device
                )

    def bulk_wait(which, source, target):
        pltpu.make_async_copy(
            target.at[pl.ds(0, 63)], target.at[pl.ds(0, 63)], bulk_sem.at[which]
        ).wait()
        pltpu.make_async_copy(
            source.at[pl.ds(0, 63)], source.at[pl.ds(0, 63)], bulk_send.at[which]
        ).wait()

    feat_copies = []
    for n, i in enumerate((-1, 1, -2, 2, -3, 3)):
        feat_copies.append(
            copy_to(feat, fbuf.at[3 - i], feat_send.at[n], feat_sem.at[n], row_peer(i))
        )
    mask_copies = []
    for i in range(1, 8):
        mask_copies.append(
            send(mask_own, mask_all.at[slab], i - 1, mask_sem.at[i - 1], slab_peer(i)[1])
        )
    mask_all[pl.ds(slab, 1)] = mask_own[...][None]
    bulk((0, k_hbm, k_ref))
    bulk((1, m_hbm, m_ref))

    fbuf[3] = feat[...]
    for copy in feat_copies:
        copy.wait()
    f_rows[14:16] = jnp.zeros((2, 8192), f32)
    for r in range(7):
        inside = jnp.logical_and(row + r >= 3, row + r < 259)
        f_rows[2 * r : 2 * r + 2] = jnp.where(inside, fbuf[r].astype(f32), 0.0)
    for dx in range(3):
        shifted = column_shift(f_rows[...], dx - 1)
        for dz in range(3):
            tap = dz * 3 + dx
            a1[16 * tap : 16 * tap + 16] = plane_shift(shifted, dz - 1).astype(bf16)

    bias_one = jnp.concatenate([b1_ref[...]] * 8, axis=1)
    bias_two = jnp.concatenate([b2_ref[...]] * 4, axis=1)
    lane = lanes((1, 256))
    hidden_row = row - 2 + jnp.minimum(lane // 32, 4)
    keep1 = jnp.where(jnp.logical_and(hidden_row >= 0, hidden_row < 256), 1.0, 0.0)
    lane = lanes((1, 128))
    hidden_row = row - 1 + jnp.minimum(lane // 32, 2)
    keep2 = jnp.where(jnp.logical_and(hidden_row >= 0, hidden_row < 256), 1.0, 0.0)
    h1e[...] = jnp.zeros_like(h1e)

    def layer_one(n, _):
        first = pl.multiple_of(n * 512, 512)
        block = lax.dot_general(
            a1[:, pl.ds(first, 512)],
            w1_ref[...],
            (((0,), (0,)), ((), ())),
            preferred_element_type=f32,
        )
        block = (jnp.maximum(block + bias_one, 0.0) * keep1).astype(bf16)
        h1m[pl.ds(pl.multiple_of(first + 128, 128), 512)] = block[:, :128]
        for dz in range(3):
            h1e[pl.ds(pl.multiple_of(first + 256 - 128 * dz, 128), 512), 32 * dz : 32 * dz + 32] = (
                block[:, 128 + 32 * dz : 160 + 32 * dz]
            )
        return 0

    lax.fori_loop(0, 16, layer_one, 0, unroll=2)
    zero = jnp.zeros((64, 128), bf16)
    h1m[0:64] = zero
    h1m[64:128] = h1m[128 + 8064 : 128 + 8128]
    h1m[128 + 8192 : 128 + 8256] = h1m[192:256]
    h1m[128 + 8256 : 128 + 8320] = zero
    h1e[128:192, 0:32] = jnp.zeros((64, 32), bf16)
    h1e[192:256, 0:32] = h1e[128 + 8064 : 128 + 8128, 32:64]
    return_rows = h1e[192:256, 32:64]
    h1e[128 + 8064 : 128 + 8128, 64:96] = return_rows
    h1e[128 + 8128 : 128 + 8192, 64:96] = jnp.zeros((64, 32), bf16)

    def layer_two(n, _):
        first = pl.multiple_of(n * 512, 512)
        low = jnp.concatenate(
            [
                h1m[pl.ds(first, 512)],
                h1m[pl.ds(pl.multiple_of(first + 128, 128), 512)],
                h1m[pl.ds(pl.multiple_of(first + 256, 128), 512)],
                h1e[pl.ds(pl.multiple_of(first + 128, 128), 512)],
            ],
            axis=1,
        )
        block = mm(low, w2_ref[...])
        column = lax.rem(lax.broadcasted_iota(jnp.int32, (512, 128), 0), 64)
        block = (
            jnp.where(column != 0, pltpu.roll(block[:, :128], 1, 0), 0.0)
            + block[:, 128:256]
            + jnp.where(column != 63, pltpu.roll(block[:, 256:], 511, 0), 0.0)
        )
        block = (jnp.maximum(block + bias_two, 0.0) * keep2).astype(bf16)
        p3[:, pl.ds(first, 512)] = lax.dot_general(
            w3_ref[...], block, (((1,), (1,)), ((), ())), preferred_element_type=f32
        )
        return 0

    lax.fori_loop(0, 16, layer_two, 0)
    total = jnp.zeros((8, 8192), f32)
    for dx in range(3):
        side = jnp.zeros((8, 8192), f32)
        for dz in range(3):
            tap = dz * 3 + dx
            side = side + plane_shift(p3[8 * tap : 8 * tap + 8], dz - 1)
        total = total + column_shift(side, dx - 1)
    for i in range(64):
        for c in range(2):
            dplanes[c, i : i + 1] = total[c : c + 1, 128 * i : 128 * i + 128]
    for c in range(2):
        turned = jnp.transpose(dplanes[c] + (cells[c] + b3_ref[c]))
        dsrc[:, c] = jnp.concatenate([turned[:64], turned[64:]], axis=1)
    bulk((2, dsrc, dbuf))
    dbuf[pl.ds(me, 1)] = dsrc[pl.ds(me, 1)]

    k_local.wait()
    for copy in table_copies:
        copy.wait()
    for copy in mask_copies:
        copy.wait()
    order = lax.broadcasted_iota(jnp.int32, (256, 256), 0)
    order = 2 * lax.rem(order, 128) + order // 128
    order = (order == lax.broadcasted_iota(jnp.int32, (256, 256), 1)).astype(bf16)
    mask_rows = mask_all[...].reshape(128, 256)
    by_line = (((1,), (1,)), ((), ()))
    mask_t[...] = lax.dot_general(order, mask_rows, by_line, preferred_element_type=f32)
    bulk_wait(0, k_hbm, k_ref)

    def put_rows(pair, even, odd):
        for h, part in ((0, even + odd), (1, even - odd)):
            for q, value in enumerate(halves(part)):
                for n in range(2):
                    first = slice(128 * n, 128 * n + 128)
                    piece = jnp.concatenate([value[:128, first], value[128:, first]], axis=1)
                    for i in range(4):
                        rows_out[q, i, 2 * pair + n, 32 * h : 32 * h + 32] = piece[
                            32 * i : 32 * i + 32
                        ]

    def adjoint_pair(pair, _):
        planes = []
        for n in range(2):
            for c in range(2):
                plane = jnp.concatenate(
                    [k_ref[8 * s + 2 * pair + n, c] for s in range(8)], axis=0
                )
                planes.append(plane * mask_rows)
        planes = lax.dot_general(
            jnp.concatenate(planes, axis=0), order, by_line, preferred_element_type=f32
        ).astype(bf16)
        sides = []
        for p in range(2):
            cell = slice(128 * p, 128 * p + 128)
            spectrum = jnp.concatenate(
                [
                    jnp.concatenate([planes[0:128, cell], planes[128:256, cell]], axis=1),
                    jnp.concatenate([planes[256:384, cell], planes[384:512, cell]], axis=1),
                ],
                axis=0,
            )
            sides.append(
                lax.dot_general(gy_ref[p, 0], spectrum, by_line, preferred_element_type=f32)
                + lax.dot_general(gy_ref[p, 1], spectrum, by_line, preferred_element_type=f32)
            )
        put_rows(pair, *sides)
        return 0

    lax.fori_loop(0, 4, adjoint_pair, 0, unroll=2)
    m_local.wait()
    bulk_wait(1, m_hbm, m_ref)

    def widen_maps(j, _):
        for c in range(2):
            for h in range(4):
                for s in range(8):
                    first = h * 64 + s * 8
                    s_ref[j, c, first : first + 8] = m_ref[8 * s + j, c, h].astype(f32)
        return 0

    lax.fori_loop(0, 8, widen_maps, 0, unroll=2)

    def maps_of(j, h):
        rows = pl.ds(pl.multiple_of(h * 64, 64), 64)
        return s_ref[j, 0, rows], s_ref[j, 1, rows]

    def image_rows(h):
        left = rows_out[0, h].reshape(512, 256), rows_out[1, h].reshape(512, 256)
        image = three(left, (gz_ref[0], gz_ref[1]))
        real_total, imag_total = 0.0, 0.0
        for j in range(8):
            real, imag = maps_of(j, h)
            a_real = image[64 * j : 64 * j + 64, :128]
            a_imag = image[64 * j : 64 * j + 64, 128:]
            real_total = real_total + (real * a_real + imag * a_imag)
            imag_total = imag_total + (real * a_imag - imag * a_real)
        return jnp.stack([real_total, imag_total])

    def reduce_scatter(step, between=lambda: None):
        copies = []
        for i in (2, 1, 3):
            t, device = g_peer(i)
            code, peak = coded(image_rows(t))
            out_code[step, i - 1] = code
            out_peak[step, i - 1] = peak
            for n, (source, target) in enumerate(((out_code, part_code), (out_peak, part_peak))):
                copies.append(
                    send(
                        source.at[step, i - 1],
                        target.at[step, i - 1],
                        13 + 2 * i + n,
                        part_sem.at[step, i - 1, n],
                        device,
                    )
                )
        between()
        total = image_rows(g)

        def finish():
            for copy in copies:
                copy.wait()
            value = total
            for i in range(3):
                value = value + decoded(part_code[step, i], part_peak[step, i])
            return value

        return finish

    def gather(step, value):
        code, peak = coded(value)
        own_code[step] = code
        own_peak[step] = peak
        copies = {}
        for i in (2, 1, 3):
            _, device = g_peer(i)
            copies[i] = [
                send(
                    source.at[step],
                    target.at[step, g],
                    13 + 2 * i + n,
                    full_sem.at[step, i - 1, n],
                    device,
                )
                for n, (source, target) in enumerate(((own_code, full_code), (own_peak, full_peak)))
            ]

        def finish(i):
            for copy in copies[i]:
                copy.wait()
            t = lax.rem(g + 4 - i, 4)
            return t, decoded(full_code[step, t], full_peak[step, t])

        return finish

    def forward_rows(h, value):
        pieces = []
        for j in range(8):
            real, imag = maps_of(j, h)
            pieces.append(
                jnp.concatenate(
                    [
                        real * value[0] - imag * value[1],
                        real * value[1] + imag * value[0],
                    ],
                    axis=1,
                )
            )
        lines = three(halves(jnp.concatenate(pieces, axis=0)), (fz_ref[0], fz_ref[1]))
        for j in range(8):
            low, high = lines[64 * j : 64 * j + 32], lines[64 * j + 32 : 64 * j + 64]
            place = slice(128 * (j % 2), 128 * (j % 2) + 128)
            for p, part in enumerate((low + high, low - high)):
                for q, piece in enumerate(halves(part)):
                    for c in range(2):
                        rows_in[q, j // 2, p, c, h, :, place] = piece[:, 128 * c : 128 * c + 128]

    def forward_pair(pair, energy):
        for p in range(2):
            mask = mask_t[128 * p : 128 * p + 128]
            mask = jnp.concatenate([mask, mask], axis=1)
            mask = jnp.concatenate([mask, mask], axis=0)
            sides = [rows_in[q, pair, p].reshape(256, 256) for q in range(2)]
            spectrum = three((fy_ref[p, 0], fy_ref[p, 1]), sides) * mask
            squares = spectrum * spectrum
            energy = energy + folded(squares[:, :128] + squares[:, 128:])
            high, low = halves(spectrum)
            spectra[pair, p, 0] = high
            spectra[pair, p, 1] = low
        return energy

    def inverse_pair(pair, _):
        sides = []
        for p in range(2):
            right = spectra[pair, p, 0], spectra[pair, p, 1]
            sides.append(three((gy_ref[p, 0], gy_ref[p, 1]), right))
        put_rows(pair, *sides)
        return 0

    here = x * 8 + k * 4 + y
    plane = [
        {"x": xs[i], "k": ks[j], "y": ys[n]}
        for n in range(4)
        for j in range(2)
        for i in range(4)
        if i or j or n
    ]

    def plane_total(step, value):
        stat_own[step, 0] = value
        stat_a[step, pl.ds(here, 1)] = value[None]
        for device in plane:
            copy_to(
                stat_own.at[step, 0],
                stat_a.at[step, here],
                stat_send.at[step],
                stat_sem_a.at[step],
                device,
            )

        def finish():
            block = stat_a.at[step, pl.ds(0, 31)]
            pltpu.make_async_copy(block, block, stat_sem_a.at[step]).wait()
            pltpu.make_async_copy(block, block, stat_send.at[step]).wait()
            value = stat_a[step, 0]
            for i in range(1, 32):
                value = value + stat_a[step, i]
            return value

        return finish

    def line_total(step, value):
        stat_own[step, 1] = value
        stat_c[step, pl.ds(line, 1)] = value[None]
        copies = []
        for i in range(1, 8):
            copies.append(
                send(
                    stat_own.at[step, 1],
                    stat_c.at[step, line],
                    7 + i,
                    stat_sem_c.at[step, i - 1],
                    line_peer(i)[1],
                )
            )

        def finish():
            for copy in copies:
                copy.wait()
            value = stat_c[step, 0]
            for i in range(1, 8):
                value = value + stat_c[step, i]
            return value

        return finish

    def norm_of(value):
        return folded((value * value).reshape(128, 128))

    def operator(step, direction):
        finish = gather(step, direction)
        norm = norm_of(direction)
        forward_rows(g, direction)
        for i in (1, 3, 2):
            forward_rows(*finish(i))
        energy = lax.fori_loop(0, 4, forward_pair, jnp.zeros((8, 128), f32), unroll=4)
        stats = [jnp.sum(value, axis=0, keepdims=True) for value in (norm, energy)]
        finish_plane = plane_total(step, jnp.concatenate(stats, axis=0))
        lax.fori_loop(0, 4, inverse_pair, 0, unroll=4)
        last = []
        image = reduce_scatter(
            step + 1, lambda: last.append(line_total(step, finish_plane()))
        )
        value = last[0]()
        norm, energy = jnp.sum(value[0:1]), jnp.sum(value[1:2])
        return norm, energy + penalty * norm, image() + penalty * direction

    right = reduce_scatter(0)()
    bulk_wait(2, dsrc, dbuf)
    right = right + penalty * jnp.stack([dbuf[:, 0], dbuf[:, 1]])
    rr, curvature, image = operator(0, right)
    alpha = rr / curvature
    residual = right - alpha * image
    fresh, curvature, second = operator(1, residual)
    growth = fresh / rr
    step_size = fresh / (curvature - growth * fresh / alpha)
    q = second + growth * image
    answer = alpha * right + step_size * (residual + growth * right)
    rest = residual - step_size * q
    for c in range(2):
        osrc[:, c] = answer[c]
        osrc[:, 2 + c] = rest[c]
    bulk((3, osrc, obuf))
    obuf[pl.ds(me, 1)] = osrc[pl.ds(me, 1)]
    bulk_wait(3, osrc, obuf)
    out_ref[0] = jnp.transpose(jnp.concatenate([obuf[:, 0], obuf[:, 1]], axis=0))
    out_ref[1] = jnp.transpose(jnp.concatenate([obuf[:, 2], obuf[:, 3]], axis=0))


def body(
    prior_image,
    coil_maps,
    kspace,
    sampling,
    weight_first,
    bias_first,
    weight_middle,
    bias_middle,
    weight_last,
    bias_last,
):
    spectrum = kspace[0].reshape(16, 256, 2, 64).transpose(3, 2, 0, 1)
    maps = coil_maps[0].reshape(4, 4, 2, 128, 2, 64).transpose(5, 4, 1, 0, 2, 3)
    maps = maps.reshape(64, 2, 4, 8, 128)

    b1 = bias_first[None]
    b2 = bias_middle[None]

    forward, backward, z_forward, z_backward = tables()
    vmem = pl.BlockSpec(memory_space=pltpu.VMEM)
    hbm = pl.BlockSpec(memory_space=pl.ANY)
    out = jax.ShapeDtypeStruct((2, 128, 128), f32)
    smem = pl.BlockSpec(memory_space=pltpu.SMEM)
    dma = pltpu.SemaphoreType.DMA
    out = pl.pallas_call(
        step_kernel,
        out_shape=out,
        in_specs=[vmem] + [hbm] * 2 + [vmem] * 6 + [smem] + [hbm] * 4,
        out_specs=vmem,
        scratch_shapes=[
            pltpu.VMEM((2, 2, 256, 256), bf16),
            pltpu.VMEM((2, 2, 256, 256), bf16),
            pltpu.VMEM((2, 256, 256), bf16),
            pltpu.VMEM((2, 256, 256), bf16),
            pltpu.VMEM((144, 256), f32),
            pltpu.VMEM((144, 256), bf16),
            pltpu.VMEM((384, 512), bf16),
            pltpu.VMEM((512, 384), bf16),
            pltpu.VMEM((72, 128), f32),
            pltpu.VMEM((72, 128), bf16),
            pltpu.VMEM((64, 2, 16, 256), bf16),
            pltpu.VMEM((64, 2, 4, 8, 128), bf16),
            pltpu.VMEM((8, 2, 256, 128), f32),
            pltpu.VMEM((2, 64, 128), f32),
            pltpu.VMEM((2, 8192), f32),
            pltpu.VMEM((2, 8192), bf16),
            pltpu.VMEM((7, 2, 8192), bf16),
            pltpu.VMEM((16, 8192), f32),
            pltpu.VMEM((144, 8192), bf16),
            pltpu.VMEM((8448, 128), bf16),
            pltpu.VMEM((8448, 128), bf16),
            pltpu.VMEM((72, 8192), f32),
            pltpu.VMEM((2, 64, 128), f32),
            pltpu.VMEM((64, 2, 128), f32),
            pltpu.VMEM((64, 2, 128), f32),
            pltpu.VMEM((64, 4, 128), f32),
            pltpu.VMEM((64, 4, 128), f32),
            pltpu.VMEM((16, 256), bf16),
            pltpu.VMEM((8, 16, 256), bf16),
            pltpu.VMEM((256, 128), f32),
            pltpu.VMEM((2, 4, 2, 2, 4, 32, 256), bf16),
            pltpu.VMEM((4, 2, 2, 256, 256), bf16),
            pltpu.VMEM((2, 4, 8, 64, 256), bf16),
            pltpu.VMEM((3, 3, 2, 64, 128), jnp.int16),
            pltpu.VMEM((3, 3, 2, 128), f32),
            pltpu.VMEM((3, 3, 2, 64, 128), jnp.int16),
            pltpu.VMEM((3, 3, 2, 128), f32),
            pltpu.VMEM((2, 2, 64, 128), jnp.int16),
            pltpu.VMEM((2, 2, 128), f32),
            pltpu.VMEM((2, 4, 2, 64, 128), jnp.int16),
            pltpu.VMEM((2, 4, 2, 128), f32),
            pltpu.VMEM((2, 32, 2, 128), f32),
            pltpu.VMEM((2, 8, 2, 128), f32),
            pltpu.VMEM((2, 2, 2, 128), f32),
            dma((22,)),
            dma((3, 3, 2)),
            dma((2, 3, 2)),
            dma((7,)),
            dma((2,)),
            dma((2,)),
            dma((2, 7)),
            dma((6,)),
            dma((6,)),
            dma((4,)),
            dma((4,)),
            dma((6,)),
        ],
        compiler_params=pltpu.CompilerParams(
            collective_id=0, has_side_effects=True, vmem_limit_bytes=60 * 1024 * 1024
        ),
    )(
        prior_image[0],
        spectrum,
        maps,
        sampling,
        weight_first.transpose(0, 1, 2, 4, 3).reshape(27, 2, 32),
        weight_middle.reshape(27, 32, 32),
        weight_last.reshape(27, 2, 32),
        b1,
        b2,
        bias_last,
        jnp.asarray(forward),
        jnp.asarray(backward),
        jnp.asarray(z_forward),
        jnp.asarray(z_backward),
    )
    return out[0:1], out[1:2]


def solution(mesh):
    torus = Mesh(mesh.devices.reshape(SIZES), AXES)
    coil = ("y", "g", "b")
    slab = ("x", "k")
    in_specs = (
        P(ALL, None, None),
        P(coil, slab, None, None),
        P(coil, slab, None, None),
        P(slab, None),
        P(),
        P(),
        P(),
        P(),
        P(),
        P(),
    )
    out_specs = (P(ALL, None, None), P(ALL, None, None))
    return jax.shard_map(body, mesh=torus, in_specs=in_specs, out_specs=out_specs, check_vma=False)
```
